128 devices in a mesh: dp: 4 (over x_lo, core), ctx: 32 (over x_hi, z, y).
Axes of the slice: x: 4 (x_hi: 2, x_lo: 2; x = x_hi * 2 + x_lo), y: 4, z: 4, core: 2. Of those that a mesh axis runs over, the one named last changes fastest.
Arguments:
- projections: bfloat16 [2, 16384, 4352], P(None, ('dp', 'ctx')), may hold values from -6 to 6
- dt_raw: bfloat16 [2, 16384, 32], P(None, ('dp', 'ctx')), may hold values from -6 to 6
- a_log: float32 [32], replicated, as said below
- dt_bias: float32 [32], replicated, may hold values from -1 to 0.5
- skip_gain: float32 [32], replicated, may hold values from 0.5 to 1.5
- norm_gain: float32 [2048], replicated, may hold values from 0.25 to 1.75
- w_out: bfloat16 [2048, 2048], replicated, may hold values from -0.125 to 0.125
- base_ids: int32 [16384], P(('dp', 'ctx')), may hold values from 0 to 4
- cotangent: bfloat16 [16384, 2048], P(('dp', 'ctx')), may hold values from -24 to 24
Outputs:
- mixed_out: bfloat16 [16384, 2048], P(('dp', 'ctx'))
- d_proj: bfloat16 [2, 16384, 4352], P(None, ('dp', 'ctx'))
- d_dt_raw: bfloat16 [2, 16384, 32], P(None, ('dp', 'ctx'))
- d_w_out: float32 [2048, 2048], P(('dp', 'ctx'))
- d_heads: float32 [3, 32], replicated
- d_gain: float32 [2048], replicated
The draws below stay inside these ranges and needn't reach their ends.
Inputs may be any that keep to these rules, and one draw needn't show every extreme that they name: `a_log`: each entry is the natural logarithm of a positive per-head rate.
All inputs are finite; a program needn't handle non-finite values.
Results may differ from the reference program's by a relative error of at most 0.0059.
Values may be sent and summed in bfloat16 or wider, within the bound.
A program may use at most 320 MiB of HBM per device.

```python
import jax
import jax.numpy as jnp
from jax import lax

D = 2048
H = 32
P_SIZE = 64
NS = 128
DI = 2048
WP = 4352
BLOCK = 128
LENGTH = 4096
TOKENS = 16384
N_DP = 4


def draw_a_log(key, part):
    pick_key, fast_key, slow_key = jax.random.split(key, 3)
    fast_share = 0.5
    is_fast = jax.random.uniform(pick_key, (H,)) < fast_share
    fast_rate = jax.random.uniform(fast_key, (H,), minval=1.0 / 30.0, maxval=1.0 / 15.0)
    slow_rate = jax.random.uniform(slow_key, (H,), minval=0.2, maxval=1.5) / LENGTH
    return jnp.log(jnp.where(is_fast, fast_rate, slow_rate)).astype(jnp.float32)


def touch_ends(entries, stream_key, smallest, top_value):
    longest = entries.shape.index(max(entries.shape))
    spots = []
    for shift in (0, 1):
        where = [jax.random.randint(jax.random.fold_in(stream_key, axis), (), 0, length) for axis, length in enumerate(entries.shape)]
        where[longest] = (where[longest] + shift) % entries.shape[longest]
        spots.append(tuple(where))
    return entries.at[spots[0]].set(smallest).at[spots[1]].set(top_value)


def spiked(values, rng, source, target, parts, factor):
    def block_of(axis_at):
        return (jnp.arange(values.shape[axis_at]) // (values.shape[axis_at] // parts)).reshape((-1,) + (1,) * (values.ndim - 1 - axis_at))

    near = jax.random.permutation(rng, parts)[block_of(target)]
    other_side = (block_of(target) + parts // 2) % parts
    return jnp.where((block_of(source) == near) | (block_of(source) == other_side), factor * values, values)


def level_of(key, extent, shards, low, largest):
    level, own = 1.0, jax.random.fold_in(key, 6)
    for position, parts in shards:
        draws = jnp.exp(jax.random.uniform(jax.random.fold_in(own, position), (parts,), jnp.float32, low / len(shards), largest / len(shards)))
        level = level * jnp.repeat(draws, extent[position] // parts).reshape([-1 if axis == position else 1 for axis in range(len(extent))])
    return level


def noise(stream_key, dims, deviation, reach, cuts=(), dtype=jnp.bfloat16):
    gain = level_of(stream_key, dims, cuts, -0.22, 0.18) if cuts else 1.0
    entries = jax.random.normal(stream_key, dims, jnp.float32) * deviation * gain
    return jnp.minimum(jnp.maximum(entries, -reach), reach).astype(dtype)


def heavy_noise(key, shape, scale, most, shards, heavy, dtype=jnp.bfloat16):
    drawn = scale * jax.random.normal(key, shape, jnp.float32)
    if shards:
        drawn = drawn * level_of(key, shape, shards, -0.22, 0.18)
    return jnp.clip(spiked(drawn, jax.random.fold_in(key, 3), *heavy), -most, most).astype(dtype)


def setup_inputs(seed: int = 0) -> dict:
    splits = jax.random.split(jax.random.key(seed), 10)
    return {
        "projections": noise(splits[0], (2, TOKENS, WP), 1.0, 6.0, ((1, 128),)),
        "dt_raw": noise(splits[1], (2, TOKENS, H), 1.0, 6.0, ((1, 128),)),
        "a_log": draw_a_log(jax.random.fold_in(splits[9], 71), 0),
        "dt_bias": jnp.clip(jax.random.uniform(splits[3], (H,), jnp.float32, -1.0, 0.5), -1.0, 0.5),
        "skip_gain": jnp.clip(jax.random.uniform(splits[4], (H,), jnp.float32, 0.5, 1.5), 0.5, 1.5),
        "norm_gain": jnp.clip(1.0 + 0.15 * jax.random.normal(splits[5], (DI,), jnp.float32), 0.25, 1.75),
        "w_out": noise(splits[6], (D, DI), DI ** -0.5, 0.125),
        "base_ids": touch_ends(jax.random.randint(splits[7], (TOKENS,), 0, 5), jax.random.fold_in(splits[7], 1), 0, 4).astype(jnp.int32),
        "cotangent": heavy_noise(splits[8], (TOKENS, D), 1.0, 24.0, ((0, 128),), (0, 1, 128, 5.5)),
    }


precise = lax.Precision.HIGHEST

def split_inputs(proj_rows, dt_rows, a_log, dt_bias):
    gate_in = proj_rows[:, :DI]
    values = proj_rows[:, DI:2 * DI].reshape(proj_rows.shape[0], H, P_SIZE)
    write_map = proj_rows[:, 2 * DI:2 * DI + NS]
    read_map = proj_rows[:, 2 * DI + NS:]
    dt_step = jax.nn.softplus(dt_rows + dt_bias)
    log_decay = -jnp.exp(a_log) * dt_step
    return (gate_in, values, write_map, read_map, dt_step, log_decay)

def to_blocks(array):
    return array.reshape((array.shape[0] // BLOCK, BLOCK) + array.shape[1:])

def block_summary(values, write_map, dt_step, log_decay):
    running = jnp.cumsum(log_decay, axis=0)
    weight = jnp.exp(running[-1][None, :] - running) * dt_step
    summary = jnp.einsum('qh,qhp,qn->hpn', weight, values, write_map, precision=precise)
    return (running[-1], summary)

def block_output(values, write_map, read_map, dt_step, log_decay, entering, skip_gain):
    running = jnp.cumsum(log_decay, axis=0)
    affinity = jnp.dot(read_map, write_map.T, precision=precise)
    head_running = running.T
    spread = head_running[:, :, None] - head_running[:, None, :]
    length_q = log_decay.shape[0]
    causal = (jnp.arange(length_q)[:, None] >= jnp.arange(length_q)[None, :])[None, :, :]
    weights = jnp.exp(jnp.where(causal, spread, -1e+30)) * affinity[None, :, :] * dt_step.T[:, None, :]
    local_part = jnp.einsum('hts,shp->thp', weights, values, precision=precise)
    carried = jnp.exp(running)[:, :, None] * jnp.einsum('tn,hpn->thp', read_map, entering, precision=precise)
    return local_part + carried + skip_gain[None, :, None] * values

def local_totals(proj_rows, dt_rows, a_log, dt_bias):
    gate_in, values, write_map, read_map, dt_step, log_decay = split_inputs(proj_rows, dt_rows, a_log, dt_bias)
    block_decay, block_state = jax.vmap(block_summary)(to_blocks(values), to_blocks(write_map), to_blocks(dt_step), to_blocks(log_decay))

    def advance(carry, entry):
        return (jnp.exp(entry[0])[:, None, None] * carry + entry[1], None)
    total_state, unused = lax.scan(advance, jnp.zeros(block_state.shape[1:], jnp.float32), (block_decay, block_state))
    return (block_decay, block_state, lax.optimization_barrier(jnp.sum(block_decay, axis=0)), total_state)

def local_outputs(proj_rows, dt_rows, a_log, dt_bias, skip_gain, norm_gain, block_decay, block_state, entering):
    gate_in, values, write_map, read_map, dt_step, log_decay = split_inputs(proj_rows, dt_rows, a_log, dt_bias)

    def advance(carry, entry):
        return (jnp.exp(entry[0])[:, None, None] * carry + entry[1], carry)
    unused, before = lax.scan(advance, entering, (block_decay, block_state))
    outputs = jax.vmap(block_output, in_axes=(0, 0, 0, 0, 0, 0, None))(to_blocks(values), to_blocks(write_map), to_blocks(read_map), to_blocks(dt_step), to_blocks(log_decay), before, skip_gain)
    heads_out = outputs.reshape(gate_in.shape)
    gated = heads_out * jax.nn.silu(gate_in)
    inv_rms = lax.rsqrt(lax.optimization_barrier(jnp.mean(gated * gated, axis=-1, keepdims=True)) + 1e-05)
    return (gated * inv_rms * norm_gain).astype(jnp.bfloat16)

def strand_normed(proj_rows, dt_rows, a_log, dt_bias, skip_gain, norm_gain):
    block_decay, block_state, unused_decay, unused_state = local_totals(proj_rows, dt_rows, a_log, dt_bias)
    entering = jnp.zeros(block_state.shape[1:], jnp.float32)
    return local_outputs(proj_rows, dt_rows, a_log, dt_bias, skip_gain, norm_gain, block_decay, block_state, entering)

def one_sequence(seq_proj, seq_dt, a_log, dt_bias, skip_gain, norm_gain, w_out, seq_ids, seq_cot):

    def forward(proj32, dt32, log_rate, bias, skip_w, gain_w):
        first = strand_normed(proj32[0], dt32[0], log_rate, bias, skip_w, gain_w)
        second = strand_normed(proj32[1], dt32[1], log_rate, bias, skip_w, gain_w)
        return (first, second)
    (normed_a, normed_b), pull = jax.vjp(forward, seq_proj.astype(jnp.float32), seq_dt.astype(jnp.float32), a_log, dt_bias, skip_gain, norm_gain)
    out_a = jnp.dot(normed_a, w_out.T, preferred_element_type=jnp.float32).astype(jnp.bfloat16)
    out_b = jnp.dot(normed_b, w_out.T, preferred_element_type=jnp.float32).astype(jnp.bfloat16)
    mixed = (out_a.astype(jnp.float32) + out_b[::-1, ::-1].astype(jnp.float32)).astype(jnp.bfloat16)
    keep = seq_cot * (seq_ids != 4).astype(jnp.bfloat16)[:, None]
    grad_b = keep[::-1, ::-1]
    d_normed_a = jnp.dot(keep, w_out, preferred_element_type=jnp.float32).astype(jnp.bfloat16)
    d_normed_b = jnp.dot(grad_b, w_out, preferred_element_type=jnp.float32).astype(jnp.bfloat16)
    d_weight = jnp.dot(keep.T, normed_a, preferred_element_type=jnp.float32) + jnp.dot(grad_b.T, normed_b, preferred_element_type=jnp.float32)
    d_proj32, d_dt32, d_alog, d_bias, d_skip, d_norm = pull((d_normed_a, d_normed_b))
    return (mixed, d_proj32.astype(jnp.bfloat16), d_dt32.astype(jnp.bfloat16), d_weight, jnp.stack([d_alog, d_bias, d_skip]), d_norm)

def reference(projections, dt_raw, a_log, dt_bias, skip_gain, norm_gain, w_out, base_ids, cotangent):
    proj_seq = jnp.swapaxes(projections.reshape(2, N_DP, LENGTH, WP), 0, 1)
    dt_seq = jnp.swapaxes(dt_raw.reshape(2, N_DP, LENGTH, H), 0, 1)
    ids_seq = base_ids.reshape(N_DP, LENGTH)
    cot_seq = cotangent.reshape(N_DP, LENGTH, D)

    def per_sequence(packed):
        return one_sequence(packed[0], packed[1], a_log, dt_bias, skip_gain, norm_gain, w_out, packed[2], packed[3])
    mixed, d_proj, d_dt, d_weight, d_heads, d_norm = lax.map(per_sequence, (proj_seq, dt_seq, ids_seq, cot_seq))
    mixed_out = mixed.reshape(TOKENS, D)
    d_proj_out = jnp.swapaxes(d_proj, 0, 1).reshape(2, TOKENS, WP)
    d_dt_out = jnp.swapaxes(d_dt, 0, 1).reshape(2, TOKENS, H)
    return (mixed_out, d_proj_out, d_dt_out, lax.optimization_barrier(jnp.sum(d_weight, axis=0)), lax.optimization_barrier(jnp.sum(d_heads, axis=0)), lax.optimization_barrier(jnp.sum(d_norm, axis=0)))
```

```python
import functools

import jax
import jax.numpy as jnp
from jax import lax
from jax.experimental import pallas as pl
from jax.experimental.pallas import tpu as pltpu
from jax.sharding import PartitionSpec as P

MESH = pl.DeviceIdType.MESH
N_CTX = 32


def scan_kernel(backward, s_ref, dec_ref, out_ref, got_dec, got, pre, send_a, recv_a, send_d, recv_d, send_b, recv_b, own_sem):
    me = lax.axis_index("ctx")
    barrier = pltpu.get_barrier_semaphore()

    def peer_of(k):
        return lax.rem(me + k, N_CTX)

    def greet(k, c):
        pl.semaphore_signal(barrier, inc=1, device_id={"ctx": peer_of(k)}, device_id_type=MESH)
        return c

    lax.fori_loop(1, N_CTX, greet, 0)
    pl.semaphore_wait(barrier, N_CTX - 1)

    def copy_a(k):
        return pltpu.make_async_remote_copy(
            src_ref=s_ref.at[peer_of(k)], dst_ref=got.at[me],
            send_sem=send_a.at[k], recv_sem=recv_a.at[k],
            device_id={"ctx": peer_of(k)}, device_id_type=MESH)

    def copy_d(k):
        return pltpu.make_async_remote_copy(
            src_ref=dec_ref.at[peer_of(k)], dst_ref=got_dec.at[me],
            send_sem=send_d.at[k], recv_sem=recv_d.at[k],
            device_id={"ctx": peer_of(k)}, device_id_type=MESH)

    def copy_b(k):
        return pltpu.make_async_remote_copy(
            src_ref=pre.at[peer_of(k)], dst_ref=out_ref.at[me],
            send_sem=send_b.at[k], recv_sem=recv_b.at[k],
            device_id={"ctx": peer_of(k)}, device_id_type=MESH)

    def start(make):
        def step(k, c):
            make(k).start()
            return c
        lax.fori_loop(1, N_CTX, step, 0)

    def finish(make):
        def step(k, c):
            make(k).wait()
            return c
        lax.fori_loop(1, N_CTX, step, 0)

    if not backward:
        start(copy_d)
    start(copy_a)
    own = pltpu.make_async_copy(s_ref.at[me], got.at[me], own_sem.at[0])
    own.start()
    if not backward:
        own_d = pltpu.make_async_copy(dec_ref.at[me], got_dec.at[me], own_sem.at[1])
        own_d.start()
        own_d.wait()
        finish(copy_d)
    own.wait()
    finish(copy_a)

    decays = dec_ref if backward else got_dec

    def fold(i, carry):
        first, second = carry
        at = N_CTX - 1 - i if backward else i
        pre[at, 0:64, :] = first.astype(jnp.bfloat16)
        pre[at, 64:128, :] = second.astype(jnp.bfloat16)
        first = decays[at, 0:1, :] * first + got[at, 0:64, :].astype(jnp.float32)
        second = decays[at, 1:2, :] * second + got[at, 64:128, :].astype(jnp.float32)
        return (first, second)

    zero = jnp.zeros((64, 128), jnp.float32)
    lax.fori_loop(0, N_CTX, fold, (zero, zero))

    start(copy_b)
    own_b = pltpu.make_async_copy(pre.at[me], out_ref.at[me], own_sem.at[2])
    own_b.start()
    own_b.wait()
    finish(copy_b)


def state_scan(summary, decay, backward):
    vmem = pl.BlockSpec(memory_space=pltpu.VMEM)
    dma = pltpu.SemaphoreType.DMA
    bf = jax.ShapeDtypeStruct((N_CTX, 128, 128), jnp.bfloat16)
    dec = jax.ShapeDtypeStruct((N_CTX, 8, 128), jnp.float32)
    scratch = [
        pltpu.VMEM((N_CTX, 128, 128), jnp.bfloat16),
        pltpu.VMEM((N_CTX, 128, 128), jnp.bfloat16),
        dma((N_CTX,)), dma((N_CTX,)), dma((N_CTX,)), dma((N_CTX,)), dma((N_CTX,)), dma((N_CTX,)),
        dma((3,)),
    ]
    params = pltpu.CompilerParams(collective_id=2 if backward else 1, has_side_effects=True)
    cost = pl.CostEstimate(flops=1000000, bytes_accessed=4000000, transcendentals=0)
    if backward:
        def kernel(s_ref, dec_ref, out_ref, *rest):
            scan_kernel(True, s_ref, dec_ref, out_ref, None, *rest)
        return pl.pallas_call(
            kernel, out_shape=bf, in_specs=[vmem, vmem], out_specs=vmem,
            scratch_shapes=scratch, compiler_params=params, cost_estimate=cost, name="scan_bwd")(summary, decay)
    return pl.pallas_call(
        functools.partial(scan_kernel, False), out_shape=(bf, dec), in_specs=[vmem, vmem], out_specs=(vmem, vmem),
        scratch_shapes=scratch, compiler_params=params, cost_estimate=cost, name="scan_fwd")(summary, decay)


CUTS = ((0, 768), (768, 1408), (1408, 2048))


def scatter_kernel(s_ref, out_ref, *scratch):
    (ra0, ra1, ra2, sa0, sa1, sa2, rb0, rb1, rb2, sb0, sb1, sb2, rc0, rc1, rc2, send_sem, recv_sem) = scratch
    dp, ctx = lax.axis_index("dp"), lax.axis_index("ctx")
    x_lo, core = dp // 2, lax.rem(dp, 2)
    x_hi, z, y = ctx // 16, lax.rem(ctx // 4, 4), lax.rem(ctx, 4)
    at = {"x": x_lo * 2 + x_hi, "z": z, "y": y}

    def peer(axis, k):
        there = lax.rem(at[axis] + k, 4)
        if axis == "y":
            return there, (dp, x_hi * 16 + z * 4 + there)
        if axis == "z":
            return there, (dp, x_hi * 16 + there * 4 + y)
        return there, ((there // 2) * 2 + core, lax.rem(there, 2) * 16 + z * 4 + y)

    barrier = pltpu.get_barrier_semaphore()
    for axis in "yzx":
        for k in (1, 2, 3):
            pl.semaphore_signal(barrier, inc=1, device_id=peer(axis, k)[1], device_id_type=MESH)
    pl.semaphore_wait(barrier, 9)

    def send(stage, part, k, axis, pick, dst):
        there, device = peer(axis, k)
        index = (stage * 3 + part) * 3 + k - 1
        copy = pltpu.make_async_remote_copy(
            src_ref=pick(there), dst_ref=dst.at[k - 1],
            send_sem=send_sem.at[index], recv_sem=recv_sem.at[index],
            device_id=device, device_id_type=MESH)
        copy.start()
        return copy

    cols = [pl.ds(a, b - a) for a, b in CUTS]
    picks_a = (
        lambda t: s_ref.at[:, :, t, :, cols[0]],
        lambda t: s_ref.at[:, t, :, :, cols[1]],
        lambda t: s_ref.at[t, :, :, :, cols[2]],
    )
    axes = (("y", "z", "x"), ("z", "x", "y"), ("x", "y", "z"))
    first = [[send(0, p, k, axes[p][0], picks_a[p], (ra0, ra1, ra2)[p]) for k in (2, 1, 3)] for p in range(3)]

    def add(mine, recv, i):
        total = mine.astype(jnp.float32)
        for k in range(3):
            total = total + recv[(k,) + i].astype(jnp.float32)
        return total

    second = []
    for p in range(3):
        for copy in first[p]:
            copy.wait()
        ra, sa = (ra0, ra1, ra2)[p], (sa0, sa1, sa2)[p]

        def body(i, c, p=p, ra=ra, sa=sa):
            a, b = i // 4, lax.rem(i, 4)
            if p == 0:
                mine = s_ref[a, b, y, :, cols[0]]
            elif p == 1:
                mine = s_ref[a, z, b, :, cols[1]]
            else:
                mine = s_ref[at["x"], a, b, :, cols[2]]
            sa[a, b] = add(mine, ra, (a, b)).astype(jnp.bfloat16)
            return c

        lax.fori_loop(0, 16, body, 0)
        pick = (lambda t: sa0.at[:, t], lambda t: sa1.at[t], lambda t: sa2.at[:, t])[p]
        second.append([send(1, p, k, axes[p][1], pick, (rb0, rb1, rb2)[p]) for k in (2, 1, 3)])
    third = []
    for p in range(3):
        for copy in second[p]:
            copy.wait()
        sa, rb, sb = (sa0, sa1, sa2)[p], (rb0, rb1, rb2)[p], (sb0, sb1, sb2)[p]
        for i in range(4):
            mine = (lambda: sa0[i, z], lambda: sa1[at["x"], i], lambda: sa2[i, y])[p]()
            sb[i] = add(mine, rb, (i,)).astype(jnp.bfloat16)
        third.append([send(2, p, k, axes[p][2], lambda t, sb=sb: sb.at[t], (rc0, rc1, rc2)[p]) for k in (2, 1, 3)])
    for p in range(3):
        for copy in third[p]:
            copy.wait()
        sb, rc = (sb0, sb1, sb2)[p], (rc0, rc1, rc2)[p]
        out_ref[:, cols[p]] = add(sb[at[axes[p][2]]], rc, ())


def weight_scatter(partial):
    vmem = pl.BlockSpec(memory_space=pltpu.VMEM)
    widths = [b - a for a, b in CUTS]
    bf = jnp.bfloat16
    scratch = [pltpu.VMEM((3, 4, 4, 16, w), bf) for w in widths]
    scratch += [pltpu.VMEM((4, 4, 16, w), bf) for w in widths]
    scratch += [pltpu.VMEM((3, 4, 16, w), bf) for w in widths]
    scratch += [pltpu.VMEM((4, 16, w), bf) for w in widths]
    scratch += [pltpu.VMEM((3, 16, w), bf) for w in widths]
    scratch += [pltpu.SemaphoreType.DMA((27,)), pltpu.SemaphoreType.DMA((27,))]
    return pl.pallas_call(
        scatter_kernel, out_shape=jax.ShapeDtypeStruct((16, 2048), jnp.float32),
        in_specs=[vmem], out_specs=vmem, scratch_shapes=scratch,
        compiler_params=pltpu.CompilerParams(collective_id=3, has_side_effects=True),
        cost_estimate=pl.CostEstimate(flops=1000000, bytes_accessed=8000000, transcendentals=0),
        name="weight_scatter")(partial)


def sum_kernel(v_ref, out_ref, plane, line, part, send_a, recv_a, send_b, recv_b, own_sem):
    dp, ctx = lax.axis_index("dp"), lax.axis_index("ctx")
    q, x_hi = lax.rem(ctx, 16), ctx // 16
    e = x_hi * 4 + dp

    def peer_a(k):
        return (dp, x_hi * 16 + lax.rem(q + k, 16))

    def peer_b(k):
        there = lax.rem(e + k, 8)
        return (lax.rem(there, 4), (there // 4) * 16 + q)

    barrier = pltpu.get_barrier_semaphore()
    for k in range(1, 16):
        pl.semaphore_signal(barrier, inc=1, device_id=peer_a(k), device_id_type=MESH)
    for k in range(1, 8):
        pl.semaphore_signal(barrier, inc=1, device_id=peer_b(k), device_id_type=MESH)
    pl.semaphore_wait(barrier, 22)

    def copy_a(k):
        return pltpu.make_async_remote_copy(
            src_ref=v_ref, dst_ref=plane.at[q], send_sem=send_a.at[k], recv_sem=recv_a.at[k],
            device_id=peer_a(k), device_id_type=MESH)

    def copy_b(k):
        return pltpu.make_async_remote_copy(
            src_ref=part, dst_ref=line.at[e], send_sem=send_b.at[k], recv_sem=recv_b.at[k],
            device_id=peer_b(k), device_id_type=MESH)

    first = [copy_a(k) for k in range(1, 16)]
    for copy in first:
        copy.start()
    plane[q] = v_ref[...]
    for copy in first:
        copy.wait()
    total = plane[0]
    for i in range(1, 16):
        total = total + plane[i]
    part[...] = total
    second = [copy_b(k) for k in range(1, 8)]
    for copy in second:
        copy.start()
    line[e] = total
    for copy in second:
        copy.wait()
    total = line[0]
    for i in range(1, 8):
        total = total + line[i]
    out_ref[...] = total


def small_sum(value):
    vmem = pl.BlockSpec(memory_space=pltpu.VMEM)
    dma = pltpu.SemaphoreType.DMA
    shape = value.shape
    return pl.pallas_call(
        sum_kernel, out_shape=jax.ShapeDtypeStruct(shape, jnp.float32), in_specs=[vmem], out_specs=vmem,
        scratch_shapes=[
            pltpu.VMEM((16,) + shape, jnp.float32), pltpu.VMEM((8,) + shape, jnp.float32),
            pltpu.VMEM(shape, jnp.float32), dma((16,)), dma((16,)), dma((8,)), dma((8,)), dma((1,))],
        compiler_params=pltpu.CompilerParams(collective_id=4, has_side_effects=True),
        cost_estimate=pl.CostEstimate(flops=100000, bytes_accessed=400000, transcendentals=0),
        name="small_sum")(value)

H = 32
P_SIZE = 64
NS = 128
DI = 2048

precise = lax.Precision.HIGHEST


def split_inputs(proj_rows, dt_rows, a_log, dt_bias):
    gate_in = proj_rows[:, :DI]
    values = proj_rows[:, DI : 2 * DI].reshape(proj_rows.shape[0], H, P_SIZE)
    write_map = proj_rows[:, 2 * DI : 2 * DI + NS]
    read_map = proj_rows[:, 2 * DI + NS :]
    dt_step = jax.nn.softplus(dt_rows + dt_bias)
    log_decay = -jnp.exp(a_log) * dt_step
    return (gate_in, values, write_map, read_map, dt_step, log_decay)


def local_totals(proj_rows, dt_rows, a_log, dt_bias):
    gate_in, values, write_map, read_map, dt_step, log_decay = split_inputs(
        proj_rows, dt_rows, a_log, dt_bias
    )
    running = jnp.cumsum(log_decay, axis=0)
    weight = jnp.exp(running[-1][None, :] - running) * dt_step
    summary = jnp.einsum("qh,qhp,qn->hpn", weight, values, write_map, precision=precise)
    return (running[-1], summary)


def local_outputs(proj_rows, dt_rows, a_log, dt_bias, skip_gain, norm_gain, entering):
    gate_in, values, write_map, read_map, dt_step, log_decay = split_inputs(
        proj_rows, dt_rows, a_log, dt_bias
    )
    running = jnp.cumsum(log_decay, axis=0)
    affinity = jnp.dot(read_map, write_map.T, precision=precise)
    head_running = running.T
    spread = head_running[:, :, None] - head_running[:, None, :]
    length_q = log_decay.shape[0]
    causal = (jnp.arange(length_q)[:, None] >= jnp.arange(length_q)[None, :])[None, :, :]
    weights = (
        jnp.exp(jnp.where(causal, spread, -1e30)) * affinity[None, :, :] * dt_step.T[:, None, :]
    )
    local_part = jnp.einsum("hts,shp->thp", weights, values, precision=precise)
    carried = jnp.exp(running)[:, :, None] * jnp.einsum(
        "tn,hpn->thp", read_map, entering, precision=precise
    )
    outputs = local_part + carried + skip_gain[None, :, None] * values
    heads_out = outputs.reshape(gate_in.shape)
    gated = heads_out * jax.nn.silu(gate_in)
    inv_rms = lax.rsqrt(jnp.mean(gated * gated, axis=-1, keepdims=True) + 1e-05)
    return (gated * inv_rms * norm_gain).astype(jnp.bfloat16)


def mirror(value):
    pairs = [(i, N_CTX - 1 - i) for i in range(N_CTX)]
    return lax.ppermute(value, "ctx", pairs)[::-1, ::-1]


def to_scan(state):
    return jnp.swapaxes(state, 0, 1).reshape(H, 2 * P_SIZE, NS).astype(jnp.bfloat16)


def from_scan(state):
    return jnp.swapaxes(state.reshape(H, 2, P_SIZE, NS), 0, 1).astype(jnp.float32)


def weight_grad(grads, normed):
    core = lax.rem(lax.axis_index("dp"), 2)
    swap = [(i, i ^ 1) for i in range(4)]
    parts = grads.reshape(256, 2, 2, 512)
    mine = lax.dynamic_index_in_dim(parts, core, 2, keepdims=False).reshape(256, 1024)
    theirs = lax.dynamic_index_in_dim(parts, 1 - core, 2, keepdims=False).reshape(256, 1024)
    grads_two = jnp.concatenate([mine, lax.ppermute(theirs, "dp", swap)], 0)
    normed_two = jnp.concatenate([normed, lax.ppermute(normed, "dp", swap)], 0)
    partial = lax.dot_general(
        grads_two, normed_two, (((0,), (0,)), ((), ())), preferred_element_type=jnp.float32
    ).astype(jnp.bfloat16)
    return weight_scatter(partial.reshape(4, 4, 4, 16, 2048))


def body(projections, dt_raw, a_log, dt_bias, skip_gain, norm_gain, w_out, base_ids, cotangent):
    keep = cotangent * (base_ids != 4).astype(jnp.bfloat16)[:, None]
    grad_b = mirror(keep)
    proj32 = projections.astype(jnp.float32)
    dt32 = dt_raw.astype(jnp.float32)
    totals_fn = jax.vmap(local_totals, in_axes=(0, 0, None, None))
    (total_decay, total_state), pull_totals = jax.vjp(totals_fn, proj32, dt32, a_log, dt_bias)
    factor = jnp.exp(total_decay)
    decay_rows = jnp.broadcast_to(
        jnp.pad(factor.T, ((0, 0), (0, 6)))[:, :, None], (N_CTX, 8, 128)
    )
    entering, decays = state_scan(to_scan(total_state), decay_rows, False)
    entering = from_scan(entering)
    outputs_fn = jax.vmap(local_outputs, in_axes=(0, 0, None, None, None, None, 0))
    normed, pull_outputs = jax.vjp(
        outputs_fn, proj32, dt32, a_log, dt_bias, skip_gain, norm_gain, entering
    )
    strand_out = jnp.einsum(
        "srk,dk->srd", normed, w_out, preferred_element_type=jnp.float32
    ).astype(jnp.bfloat16)
    mixed_out = (
        strand_out[0].astype(jnp.float32) + mirror(strand_out[1]).astype(jnp.float32)
    ).astype(jnp.bfloat16)
    d_out = jnp.stack([keep, grad_b])
    d_normed = jnp.einsum("srd,dk->srk", d_out, w_out, preferred_element_type=jnp.float32).astype(
        jnp.bfloat16
    )
    d_proj_b, d_dt_b, d_alog_b, d_bias_b, d_skip, d_norm, d_entering = pull_outputs(d_normed)
    d_total_state = from_scan(state_scan(to_scan(d_entering), decays, True))
    d_total_decay = factor * jnp.sum(entering * d_total_state, axis=(-2, -1))
    d_w_out = weight_grad(d_out.reshape(256, 2048), normed.reshape(256, 2048))
    d_proj_a, d_dt_a, d_alog_a, d_bias_a = pull_totals((d_total_decay, d_total_state))
    d_proj_all = (d_proj_a + d_proj_b).astype(jnp.bfloat16)
    d_dt_all = (d_dt_a + d_dt_b).astype(jnp.bfloat16)
    heads = jnp.concatenate([d_alog_a + d_alog_b, d_bias_a + d_bias_b, d_skip])
    packed = jnp.concatenate([d_norm, jnp.pad(heads, (0, 1024 - 96))]).reshape(24, 128)
    summed = small_sum(packed).reshape(-1)
    return (
        mixed_out,
        d_proj_all,
        d_dt_all,
        d_w_out,
        summed[2048 : 2048 + 96].reshape(3, 32),
        summed[:2048],
    )


def solution(mesh):
    placed = (
        P(None, ("dp", "ctx"), None),
        P(None, ("dp", "ctx"), None),
        P(),
        P(),
        P(),
        P(),
        P(),
        P(("dp", "ctx")),
        P(("dp", "ctx"), None),
    )
    return jax.shard_map(
        body,
        mesh=mesh,
        in_specs=placed,
        out_specs=(
            P(("dp", "ctx"), None),
            P(None, ("dp", "ctx"), None),
            P(None, ("dp", "ctx"), None),
            P(("dp", "ctx"), None),
            P(),
            P(),
        ),
        check_vma=False,
    )
```

```python
import functools

import jax
import jax.numpy as jnp
from jax import lax
from jax.experimental import pallas as pl
from jax.experimental.pallas import tpu as pltpu
from jax.sharding import PartitionSpec as P

MESH = pl.DeviceIdType.MESH
N_CTX = 32


def scan_kernel(backward, s_ref, dec_ref, out_ref, got_dec, got, pre, send_a, recv_a, send_d, recv_d, send_b, recv_b, own_sem):
    me = lax.axis_index("ctx")
    barrier = pltpu.get_barrier_semaphore()

    def peer_of(k):
        return lax.rem(me + k, N_CTX)

    def greet(k, c):
        pl.semaphore_signal(barrier, inc=1, device_id={"ctx": peer_of(k)}, device_id_type=MESH)
        return c

    lax.fori_loop(1, N_CTX, greet, 0)
    pl.semaphore_wait(barrier, N_CTX - 1)

    def copy_a(k):
        return pltpu.make_async_remote_copy(
            src_ref=s_ref.at[peer_of(k)], dst_ref=got.at[me],
            send_sem=send_a.at[k], recv_sem=recv_a.at[k],
            device_id={"ctx": peer_of(k)}, device_id_type=MESH)

    def copy_d(k):
        return pltpu.make_async_remote_copy(
            src_ref=dec_ref.at[peer_of(k)], dst_ref=got_dec.at[me],
            send_sem=send_d.at[k], recv_sem=recv_d.at[k],
            device_id={"ctx": peer_of(k)}, device_id_type=MESH)

    def copy_b(k):
        return pltpu.make_async_remote_copy(
            src_ref=pre.at[peer_of(k)], dst_ref=out_ref.at[me],
            send_sem=send_b.at[k], recv_sem=recv_b.at[k],
            device_id={"ctx": peer_of(k)}, device_id_type=MESH)

    def start(make):
        def step(k, c):
            make(k).start()
            return c
        lax.fori_loop(1, N_CTX, step, 0)

    def finish(make):
        def step(k, c):
            make(k).wait()
            return c
        lax.fori_loop(1, N_CTX, step, 0)

    if not backward:
        start(copy_d)
    start(copy_a)
    own = pltpu.make_async_copy(s_ref.at[me], got.at[me], own_sem.at[0])
    own.start()
    if not backward:
        own_d = pltpu.make_async_copy(dec_ref.at[me], got_dec.at[me], own_sem.at[1])
        own_d.start()
        own_d.wait()
        finish(copy_d)
    own.wait()
    finish(copy_a)

    decays = dec_ref if backward else got_dec

    def fold(i, carry):
        first, second = carry
        at = N_CTX - 1 - i if backward else i
        pre[at, 0:64, :] = first.astype(jnp.bfloat16)
        pre[at, 64:128, :] = second.astype(jnp.bfloat16)
        first = decays[at, 0:1, :] * first + got[at, 0:64, :].astype(jnp.float32)
        second = decays[at, 8:9, :] * second + got[at, 64:128, :].astype(jnp.float32)
        return (first, second)

    zero = jnp.zeros((64, 128), jnp.float32)
    lax.fori_loop(0, N_CTX, fold, (zero, zero))

    start(copy_b)
    own_b = pltpu.make_async_copy(pre.at[me], out_ref.at[me], own_sem.at[2])
    own_b.start()
    own_b.wait()
    finish(copy_b)


def state_scan(summary, decay, backward):
    vmem = pl.BlockSpec(memory_space=pltpu.VMEM)
    dma = pltpu.SemaphoreType.DMA
    bf = jax.ShapeDtypeStruct((N_CTX, 128, 128), jnp.bfloat16)
    dec = jax.ShapeDtypeStruct((N_CTX, 16, 128), jnp.float32)
    scratch = [
        pltpu.VMEM((N_CTX, 128, 128), jnp.bfloat16),
        pltpu.VMEM((N_CTX, 128, 128), jnp.bfloat16),
        dma((N_CTX,)), dma((N_CTX,)), dma((N_CTX,)), dma((N_CTX,)), dma((N_CTX,)), dma((N_CTX,)),
        dma((3,)),
    ]
    params = pltpu.CompilerParams(collective_id=2 if backward else 1, has_side_effects=True)
    cost = pl.CostEstimate(flops=1000000, bytes_accessed=4000000, transcendentals=0)
    if backward:
        def kernel(s_ref, dec_ref, out_ref, *rest):
            scan_kernel(True, s_ref, dec_ref, out_ref, None, *rest)
        return pl.pallas_call(
            kernel, out_shape=bf, in_specs=[vmem, vmem], out_specs=vmem,
            scratch_shapes=scratch, compiler_params=params, cost_estimate=cost, name="scan_bwd")(summary, decay)
    return pl.pallas_call(
        functools.partial(scan_kernel, False), out_shape=(bf, dec), in_specs=[vmem, vmem], out_specs=(vmem, vmem),
        scratch_shapes=scratch, compiler_params=params, cost_estimate=cost, name="scan_fwd")(summary, decay)


CUTS = ((0, 768), (768, 1408), (1408, 2048))


def scatter_kernel(s_ref, out_ref, *scratch):
    (ra0, ra1, ra2, sa0, sa1, sa2, rb0, rb1, rb2, sb0, sb1, sb2, rc0, rc1, rc2, send_sem, recv_sem) = scratch
    dp, ctx = lax.axis_index("dp"), lax.axis_index("ctx")
    x_lo, core = dp // 2, lax.rem(dp, 2)
    x_hi, z, y = ctx // 16, lax.rem(ctx // 4, 4), lax.rem(ctx, 4)
    at = {"x": x_lo * 2 + x_hi, "z": z, "y": y}

    def peer(axis, k):
        there = lax.rem(at[axis] + k, 4)
        if axis == "y":
            return there, (dp, x_hi * 16 + z * 4 + there)
        if axis == "z":
            return there, (dp, x_hi * 16 + there * 4 + y)
        return there, ((there // 2) * 2 + core, lax.rem(there, 2) * 16 + z * 4 + y)

    barrier = pltpu.get_barrier_semaphore()
    for axis in "yzx":
        for k in (1, 2, 3):
            pl.semaphore_signal(barrier, inc=1, device_id=peer(axis, k)[1], device_id_type=MESH)
    pl.semaphore_wait(barrier, 9)

    def send(stage, part, k, axis, pick, dst):
        there, device = peer(axis, k)
        index = (stage * 3 + part) * 3 + k - 1
        copy = pltpu.make_async_remote_copy(
            src_ref=pick(there), dst_ref=dst.at[k - 1],
            send_sem=send_sem.at[index], recv_sem=recv_sem.at[index],
            device_id=device, device_id_type=MESH)
        copy.start()
        return copy

    cols = [pl.ds(a, b - a) for a, b in CUTS]
    picks_a = (
        lambda t: s_ref.at[:, :, t, :, cols[0]],
        lambda t: s_ref.at[:, t, :, :, cols[1]],
        lambda t: s_ref.at[t, :, :, :, cols[2]],
    )
    axes = (("y", "z", "x"), ("z", "x", "y"), ("x", "y", "z"))
    first = [[send(0, p, k, axes[p][0], picks_a[p], (ra0, ra1, ra2)[p]) for k in (2, 1, 3)] for p in range(3)]

    def add(mine, recv, i):
        total = mine.astype(jnp.float32)
        for k in range(3):
            total = total + recv[(k,) + i].astype(jnp.float32)
        return total

    second = []
    for p in range(3):
        for copy in first[p]:
            copy.wait()
        ra, sa = (ra0, ra1, ra2)[p], (sa0, sa1, sa2)[p]

        def body(i, c, p=p, ra=ra, sa=sa):
            a, b = i // 4, lax.rem(i, 4)
            if p == 0:
                mine = s_ref[a, b, y, :, cols[0]]
            elif p == 1:
                mine = s_ref[a, z, b, :, cols[1]]
            else:
                mine = s_ref[at["x"], a, b, :, cols[2]]
            sa[a, b] = add(mine, ra, (a, b)).astype(jnp.bfloat16)
            return c

        lax.fori_loop(0, 16, body, 0)
        pick = (lambda t: sa0.at[:, t], lambda t: sa1.at[t], lambda t: sa2.at[:, t])[p]
        second.append([send(1, p, k, axes[p][1], pick, (rb0, rb1, rb2)[p]) for k in (2, 1, 3)])
    third = []
    for p in range(3):
        for copy in second[p]:
            copy.wait()
        sa, rb, sb = (sa0, sa1, sa2)[p], (rb0, rb1, rb2)[p], (sb0, sb1, sb2)[p]
        for i in range(4):
            mine = (lambda: sa0[i, z], lambda: sa1[at["x"], i], lambda: sa2[i, y])[p]()
            sb[i] = add(mine, rb, (i,)).astype(jnp.bfloat16)
        third.append([send(2, p, k, axes[p][2], lambda t, sb=sb: sb.at[t], (rc0, rc1, rc2)[p]) for k in (2, 1, 3)])
    for p in range(3):
        for copy in third[p]:
            copy.wait()
        sb, rc = (sb0, sb1, sb2)[p], (rc0, rc1, rc2)[p]
        out_ref[:, cols[p]] = add(sb[at[axes[p][2]]], rc, ())


def weight_scatter(partial):
    vmem = pl.BlockSpec(memory_space=pltpu.VMEM)
    widths = [b - a for a, b in CUTS]
    bf = jnp.bfloat16
    scratch = [pltpu.VMEM((3, 4, 4, 16, w), bf) for w in widths]
    scratch += [pltpu.VMEM((4, 4, 16, w), bf) for w in widths]
    scratch += [pltpu.VMEM((3, 4, 16, w), bf) for w in widths]
    scratch += [pltpu.VMEM((4, 16, w), bf) for w in widths]
    scratch += [pltpu.VMEM((3, 16, w), bf) for w in widths]
    scratch += [pltpu.SemaphoreType.DMA((27,)), pltpu.SemaphoreType.DMA((27,))]
    return pl.pallas_call(
        scatter_kernel, out_shape=jax.ShapeDtypeStruct((16, 2048), jnp.float32),
        in_specs=[vmem], out_specs=vmem, scratch_shapes=scratch,
        compiler_params=pltpu.CompilerParams(collective_id=3, has_side_effects=True),
        cost_estimate=pl.CostEstimate(flops=1000000, bytes_accessed=8000000, transcendentals=0),
        name="weight_scatter")(partial)


def sum_kernel(v_ref, out_ref, plane, line, part, send_a, recv_a, send_b, recv_b, own_sem):
    dp, ctx = lax.axis_index("dp"), lax.axis_index("ctx")
    q, x_hi = lax.rem(ctx, 16), ctx // 16
    e = x_hi * 4 + dp

    def peer_a(k):
        return (dp, x_hi * 16 + lax.rem(q + k, 16))

    def peer_b(k):
        there = lax.rem(e + k, 8)
        return (lax.rem(there, 4), (there // 4) * 16 + q)

    barrier = pltpu.get_barrier_semaphore()
    for k in range(1, 16):
        pl.semaphore_signal(barrier, inc=1, device_id=peer_a(k), device_id_type=MESH)
    for k in range(1, 8):
        pl.semaphore_signal(barrier, inc=1, device_id=peer_b(k), device_id_type=MESH)
    pl.semaphore_wait(barrier, 22)

    def copy_a(k):
        return pltpu.make_async_remote_copy(
            src_ref=v_ref, dst_ref=plane.at[q], send_sem=send_a.at[k], recv_sem=recv_a.at[k],
            device_id=peer_a(k), device_id_type=MESH)

    def copy_b(k):
        return pltpu.make_async_remote_copy(
            src_ref=part, dst_ref=line.at[e], send_sem=send_b.at[k], recv_sem=recv_b.at[k],
            device_id=peer_b(k), device_id_type=MESH)

    first = [copy_a(k) for k in range(1, 16)]
    for copy in first:
        copy.start()
    plane[q] = v_ref[...]
    for copy in first:
        copy.wait()
    total = plane[0]
    for i in range(1, 16):
        total = total + plane[i]
    part[...] = total
    second = [copy_b(k) for k in range(1, 8)]
    for copy in second:
        copy.start()
    line[e] = total
    for copy in second:
        copy.wait()
    total = line[0]
    for i in range(1, 8):
        total = total + line[i]
    out_ref[...] = total


def small_sum(value):
    vmem = pl.BlockSpec(memory_space=pltpu.VMEM)
    dma = pltpu.SemaphoreType.DMA
    shape = value.shape
    return pl.pallas_call(
        sum_kernel, out_shape=jax.ShapeDtypeStruct(shape, jnp.float32), in_specs=[vmem], out_specs=vmem,
        scratch_shapes=[
            pltpu.VMEM((16,) + shape, jnp.float32), pltpu.VMEM((8,) + shape, jnp.float32),
            pltpu.VMEM(shape, jnp.float32), dma((16,)), dma((16,)), dma((8,)), dma((8,)), dma((1,))],
        compiler_params=pltpu.CompilerParams(collective_id=4, has_side_effects=True),
        cost_estimate=pl.CostEstimate(flops=100000, bytes_accessed=400000, transcendentals=0),
        name="small_sum")(value)

H = 32
P_SIZE = 64
NS = 128
DI = 2048
Q = 128
PAIRS = 16
B_AT = 2 * DI
C_AT = 2 * DI + NS
bf16 = jnp.bfloat16
f32 = jnp.float32
precise = lax.Precision.HIGHEST


def dot(a, b, dims=((1,), (0,)), precision=None):
    return lax.dot_general(a, b, (dims, ((), ())), precision=precision, preferred_element_type=f32)


ROWS = ((0,), (0,))
LANES = ((1,), (1,))


def iota(shape, axis):
    return lax.broadcasted_iota(jnp.int32, shape, axis)


def head_map():
    return (iota((H, DI), 0) == iota((H, DI), 1) // P_SIZE).astype(f32).astype(bf16)


def expand(value, heads):
    high = value.astype(bf16)
    low = (value - high.astype(f32)).astype(bf16)
    return dot(high, heads) + dot(low, heads)


def per_head(value, heads):
    return dot(value.astype(bf16), heads, LANES)


def softplus(value):
    return jnp.maximum(value, 0.0) + jnp.log1p(jnp.exp(-jnp.abs(value)))


def sigmoid(value):
    return 1.0 / (1.0 + jnp.exp(-value))


def tril():
    return iota((Q, Q), 0) >= iota((Q, Q), 1)


def half_masks():
    left = (iota((Q, 128), 1) < P_SIZE).astype(f32)
    return left.astype(bf16), (1.0 - left).astype(bf16)


def summary_kernel(proj, dt_raw, dt_raw_t, rate, bias, rate_t, bias_t, state, decay, dt_out, run_out, dt_t_out, run_t_out):
    lower = tril().astype(f32)
    dt = softplus(dt_raw[0].astype(f32) + bias[...])
    run = dot(lower, -rate[...] * dt, precision=precise)
    dt_t = softplus(dt_raw_t[0].astype(f32) + bias_t[...])
    run_t = dot(-rate_t[...] * dt_t, lower, LANES, precision=precise)
    dt_out[0] = dt
    run_out[0] = run
    dt_t_out[0] = dt_t
    run_t_out[0] = run_t
    weight = jnp.exp(run[Q - 1 : Q, :] - run) * dt
    weighed = (expand(weight, head_map()) * proj[0, :, DI:B_AT].astype(f32)).astype(bf16)
    total = dot(weighed, proj[0, :, B_AT:C_AT], ROWS)
    state[...] = total.astype(bf16).reshape(H, P_SIZE, NS)
    left = jnp.exp(run_t[:, Q - 1 : Q])
    for h in range(H):
        decay[h] = jnp.broadcast_to(left[h : h + 1, :], (8, 128))


def forward_kernel(proj, dt_raw_unused, run, dt_t, run_t, entering, skip, gain, normed, y_out, spread_out, mix_out, local):
    write, read = proj[0, :, B_AT:C_AT], proj[0, :, C_AT:]
    affinity = dot(read, write, LANES)
    affinity = jnp.concatenate([affinity, affinity], 1)
    causal = tril()
    left, right = half_masks()
    for j in range(PAIRS):
        cols = slice(DI + 128 * j, DI + 128 * j + 128)
        both = []
        for h in (2 * j, 2 * j + 1):
            gap = run[0, :, h : h + 1] - run_t[0, h : h + 1, :]
            both.append(jnp.exp(jnp.where(causal, gap, -1e30)) * dt_t[0, h : h + 1, :])
        spread = jnp.concatenate(both, 1)
        spread_out[0, j] = spread.astype(bf16)
        values = proj[0, :, cols]
        stacked = jnp.concatenate([values * left, values * right], 0)
        mixing = (spread * affinity).astype(bf16)
        mix_out[0, j] = mixing
        local[:, 128 * j : 128 * j + 128] = dot(mixing, stacked)
    carried = dot(read, entering[...].reshape(DI, NS), LANES)
    grown = expand(jnp.exp(run[0]), head_map())
    y = local[...] + grown * carried + skip[...] * proj[0, :, DI:B_AT].astype(f32)
    y_out[0] = y
    gate = proj[0, :, :DI].astype(f32)
    gated = y * gate * sigmoid(gate)
    inv = lax.rsqrt(jnp.mean(gated * gated, axis=1, keepdims=True) + 1e-05)
    normed[0] = (gated * inv * gain[...]).astype(bf16)


def backward_kernel(proj, y_in, d_normed, run, spread_in, mix_in, entering, skip, gain,
                    d_gate, d_x, d_entering, d_write, d_read, gains, from_y, from_x, dy_keep, dx_keep):
    heads = head_map()
    gate = proj[0, :, :DI].astype(f32)
    y = y_in[0]
    sig = sigmoid(gate)
    silu = gate * sig
    gated = y * silu
    inv = lax.rsqrt(jnp.mean(gated * gated, axis=1, keepdims=True) + 1e-05)
    dn = d_normed[0].astype(f32)
    gains[0, 0:1, :] = jnp.sum(dn * (gated * inv), axis=0, keepdims=True)
    up = dn * gain[...]
    pull = jnp.mean(up * gated, axis=1, keepdims=True) * (inv * inv * inv)
    d_gated = inv * up - gated * pull
    dy = d_gated * silu
    d_gate[0] = (d_gated * y * (sig * (1.0 + gate * (1.0 - sig)))).astype(bf16)
    values = proj[0, :, DI:B_AT].astype(f32)
    gains[0, 1:2, :] = jnp.sum(dy * values, axis=0, keepdims=True)
    dy_keep[...] = dy.astype(bf16)
    from_y[0] = per_head(dy_keep[...].astype(f32) * (y - skip[...] * values), heads)
    grown = (expand(jnp.exp(run[0]), heads) * dy).astype(bf16)
    write, read = proj[0, :, B_AT:C_AT], proj[0, :, C_AT:]
    state = entering[...].reshape(DI, NS)
    d_entering[...] = dot(grown, read, ROWS).astype(bf16).reshape(H, P_SIZE, NS)
    d_c = dot(grown, state)
    left, right = half_masks()
    first = iota((Q, 128), 1) < P_SIZE
    d_aff = jnp.zeros((Q, Q), f32)
    for j in range(PAIRS):
        cols = slice(128 * j, 128 * j + 128)
        dyp = dy_keep[:, cols]
        x = proj[0, :, DI + 128 * j : DI + 128 * j + 128]
        stacked = jnp.concatenate([x * left, x * right], 0)
        d_mix = dot(dyp, stacked, LANES) * spread_in[0, j].astype(f32)
        d_aff = d_aff + d_mix[:, :Q] + d_mix[:, Q:]
        back = dot(mix_in[0, j], dyp, ROWS)
        dx_keep[:, cols] = jnp.where(first, back[:Q], back[Q:])
    d_aff = d_aff.astype(bf16)
    d_read[0] = (d_c + dot(d_aff, write)).astype(bf16)
    d_write[0] = dot(d_aff, read, ROWS)
    dx = dx_keep[...]
    from_x[0] = per_head(values * dx, heads)
    d_x[0] = dx + skip[...] * dy


def finish_kernel(proj, dt_raw, dt_in, run_in, leaving, entering, from_y, from_x, d_x, d_gate, d_write, d_read,
                  rate, bias, d_proj, d_dt, sums):
    heads = head_map()
    dt, run = dt_in[0], run_in[0]
    last = run[Q - 1 : Q, :]
    weight = expand(jnp.exp(last - run) * dt, heads)
    values = proj[0, :, DI:B_AT].astype(f32)
    out = leaving[...].reshape(DI, NS)
    d_state = weight * dot(proj[0, :, B_AT:C_AT], out, LANES)
    d_b = d_write[0] + dot((weight * values).astype(bf16), out)
    d_proj[0, :, :DI] = d_gate[0]
    d_proj[0, :, DI:B_AT] = (d_x[0] + d_state).astype(bf16)
    d_proj[0, :, B_AT:C_AT] = d_b.astype(bf16)
    d_proj[0, :, C_AT:] = d_read[0]
    from_state = per_head(values * d_state, heads)
    total = from_x[0] + from_state
    meet = jnp.sum(entering[...].astype(f32) * leaving[...].astype(f32), axis=1)
    meet = dot(jnp.ones((8, NS), f32), meet, LANES, precision=precise)[0:1, :]
    d_last = jnp.exp(last) * meet + jnp.sum(from_state, axis=0, keepdims=True)
    upper = (iota((Q, Q), 0) <= iota((Q, Q), 1)).astype(f32)
    d_log = dot(upper, from_y[0] - total, precision=precise) + d_last
    d_step = total / dt - rate[...] * d_log
    d_raw = d_step * sigmoid(dt_raw[0].astype(f32) + bias[...])
    d_dt[0] = d_raw.astype(bf16)
    sums[0, 0:1, :] = jnp.sum(d_log * (-rate[...] * dt), axis=0, keepdims=True)
    sums[0, 1:2, :] = jnp.sum(d_raw, axis=0, keepdims=True)


def strand(*shape):
    return pl.BlockSpec((1,) + shape, lambda s: (s,) + (0,) * len(shape))


def shared(*shape):
    return pl.BlockSpec(shape, lambda s: (0,) * len(shape))


STATE = pl.BlockSpec((H, P_SIZE, NS), lambda s: (0, s, 0))


def like(dtype, *shape):
    return jax.ShapeDtypeStruct(shape, dtype)


def strand_call(kernel, name, in_specs, out_specs, out_shape, scratch=(), flops=2000000000):
    return pl.pallas_call(
        kernel, grid=(2,), in_specs=in_specs, out_specs=out_specs, out_shape=out_shape,
        scratch_shapes=list(scratch), name=name,
        cost_estimate=pl.CostEstimate(flops=flops, bytes_accessed=10000000, transcendentals=0))


def flipped(block):
    turn = (iota((128, 128), 0) + iota((128, 128), 1) == 127).astype(f32).astype(bf16)
    rows = dot(turn, block).astype(bf16)
    parts = [dot(rows[:, 128 * j : 128 * j + 128], turn) for j in range(15, -1, -1)]
    return jnp.concatenate(parts, 1)


def flip_kernel(keep, got, out):
    out[0] = keep[...]
    out[1] = flipped(got[...]).astype(bf16)


def mix_kernel(own, got, out):
    out[...] = (own[...].astype(f32) + flipped(got[...])).astype(bf16)


def whole_call(kernel, name, out_shape, *args):
    vmem = pl.BlockSpec(memory_space=pltpu.VMEM)
    return pl.pallas_call(
        kernel, out_shape=out_shape, in_specs=[vmem] * len(args), out_specs=vmem, name=name,
        cost_estimate=pl.CostEstimate(flops=200000000, bytes_accessed=2000000, transcendentals=0))(*args)


def mirror(value):
    return lax.ppermute(value, "ctx", [(i, N_CTX - 1 - i) for i in range(N_CTX)])


def weight_grad(grads, normed):
    core = lax.rem(lax.axis_index("dp"), 2)
    swap = [(i, i ^ 1) for i in range(4)]
    parts = grads.reshape(256, 2, 2, 512)
    mine = lax.dynamic_index_in_dim(parts, core, 2, keepdims=False).reshape(256, 1024)
    theirs = lax.dynamic_index_in_dim(parts, 1 - core, 2, keepdims=False).reshape(256, 1024)
    grads_two = jnp.concatenate([mine, lax.ppermute(theirs, "dp", swap)], 0)
    normed_two = jnp.concatenate([normed, lax.ppermute(normed, "dp", swap)], 0)
    partial = lax.dot_general(
        grads_two, normed_two, (((0,), (0,)), ((), ())), preferred_element_type=f32
    ).astype(bf16)
    return weight_scatter(partial.reshape(4, 4, 4, 16, DI))


def body(projections, dt_raw, a_log, dt_bias, skip_gain, norm_gain, w_out, base_ids, cotangent):
    keep = cotangent * (base_ids != 4).astype(bf16)[:, None]
    d_out = whole_call(flip_kernel, "flip_keep", like(bf16, 2, Q, DI), keep, mirror(keep))
    rate = jnp.exp(a_log)
    proj, tok = strand(Q, 2 * DI + 2 * NS), strand(Q, H)
    tok_t, wide = strand(H, Q), strand(Q, DI)
    row, col, lane = shared(1, H), shared(H, 1), shared(1, DI)
    skip, gain = jnp.repeat(skip_gain, P_SIZE)[None], norm_gain[None]
    state, factor, dt, run, dt_t, run_t = strand_call(
        summary_kernel, "summary", [proj, tok, tok_t, row, row, col, col],
        [STATE, pl.BlockSpec((H, 8, NS), lambda s: (0, s, 0)), tok, tok, tok_t, tok_t],
        [like(bf16, H, 2 * P_SIZE, NS), like(f32, H, 16, NS), like(f32, 2, Q, H), like(f32, 2, Q, H),
         like(f32, 2, H, Q), like(f32, 2, H, Q)],
    )(projections, dt_raw, jnp.swapaxes(dt_raw, 1, 2), rate[None], dt_bias[None], rate[:, None], dt_bias[:, None])
    entering, decays = state_scan(state, factor, False)
    spread_spec = strand(PAIRS, Q, 2 * Q)
    normed, y, spread, mixing = strand_call(
        forward_kernel, "forward", [proj, tok, tok, tok_t, tok_t, STATE, lane, lane],
        [wide, wide, spread_spec, spread_spec],
        [like(bf16, 2, Q, DI), like(f32, 2, Q, DI), like(bf16, 2, PAIRS, Q, 2 * Q),
         like(bf16, 2, PAIRS, Q, 2 * Q)],
        [pltpu.VMEM((Q, DI), f32)],
    )(projections, dt_raw, run, dt_t, run_t, entering, skip, gain)
    strand_out = jnp.einsum("srk,dk->srd", normed, w_out, preferred_element_type=f32).astype(bf16)
    moved = mirror(strand_out[1])
    d_normed = jnp.einsum("srd,dk->srk", d_out, w_out, preferred_element_type=f32).astype(bf16)
    d_gate, d_x, d_entering, d_write, d_read, gains, from_y, from_x = strand_call(
        backward_kernel, "backward", [proj, wide, wide, tok, spread_spec, spread_spec, STATE, lane, lane],
        [wide, wide, STATE, strand(Q, NS), strand(Q, NS), strand(2, DI), tok, tok],
        [like(bf16, 2, Q, DI), like(f32, 2, Q, DI), like(bf16, H, 2 * P_SIZE, NS), like(f32, 2, Q, NS),
         like(bf16, 2, Q, NS), like(f32, 2, 2, DI), like(f32, 2, Q, H), like(f32, 2, Q, H)],
        [pltpu.VMEM((Q, DI), bf16), pltpu.VMEM((Q, DI), f32)],
    )(projections, y, d_normed, run, spread, mixing, entering, skip, gain)
    leaving = state_scan(d_entering, decays, True)
    d_w_out = weight_grad(d_out.reshape(2 * Q, DI), normed.reshape(2 * Q, DI))
    mixed_out = whole_call(mix_kernel, "mix", like(bf16, Q, DI), strand_out[0], moved)
    d_proj, d_dt, sums = strand_call(
        finish_kernel, "finish",
        [proj, tok, tok, tok, STATE, STATE, tok, tok, wide, wide, strand(Q, NS), strand(Q, NS), row, row],
        [proj, tok, strand(2, H)],
        [like(bf16, 2, Q, 2 * DI + 2 * NS), like(bf16, 2, Q, H), like(f32, 2, 2, H)],
    )(projections, dt_raw, dt, run, leaving, entering, from_y, from_x, d_x, d_gate, d_write, d_read,
      rate[None], dt_bias[None])
    gains = jnp.sum(gains, axis=0)
    d_skip = jnp.sum(gains[1].reshape(H, P_SIZE), axis=1)
    small = jnp.concatenate([gains[0], jnp.sum(sums, axis=0).reshape(-1), d_skip, jnp.zeros((928,), f32)])
    summed = small_sum(small.reshape(24, 128)).reshape(-1)
    return (mixed_out, d_proj, d_dt, d_w_out, summed[2048 : 2048 + 96].reshape(3, 32), summed[:2048])


def solution(mesh):
    placed = (
        P(None, ("dp", "ctx"), None),
        P(None, ("dp", "ctx"), None),
        P(),
        P(),
        P(),
        P(),
        P(),
        P(("dp", "ctx")),
        P(("dp", "ctx"), None),
    )
    return jax.shard_map(
        body,
        mesh=mesh,
        in_specs=placed,
        out_specs=(
            P(("dp", "ctx"), None),
            P(None, ("dp", "ctx"), None),
            P(None, ("dp", "ctx"), None),
            P(("dp", "ctx"), None),
            P(),
            P(),
        ),
        check_vma=False,
    )
```

```python
import functools

import jax
import jax.numpy as jnp
from jax import lax
from jax.experimental import pallas as pl
from jax.experimental.pallas import tpu as pltpu
from jax.sharding import PartitionSpec as P

MESH = pl.DeviceIdType.MESH
N_CTX = 32


CUTS = ((0, 768), (768, 1408), (1408, 2048))


def place():
    dp, ctx = lax.axis_index("dp"), lax.axis_index("ctx")
    x_lo, core = dp // 2, lax.rem(dp, 2)
    x_hi, z, y = ctx // 16, lax.rem(ctx // 4, 4), lax.rem(ctx, 4)
    return dp, core, {"x": x_lo * 2 + x_hi, "z": z, "y": y}


def line_peer(axis, k):
    dp, core, at = place()
    there = lax.rem(at[axis] + k, 4)
    x = there if axis == "x" else at["x"]
    z = there if axis == "z" else at["z"]
    y = there if axis == "y" else at["y"]
    return there, ((x // 2) * 2 + core, lax.rem(x, 2) * 16 + z * 4 + y)


def scatter_steps(s_ref, out_ref, scratch):
    (ra0, ra1, ra2, sa0, sa1, sa2, rb0, rb1, rb2, sb0, sb1, sb2, rc0, rc1, rc2, send_sem, recv_sem) = scratch
    _, _, at = place()
    cols = [pl.ds(a, b - a) for a, b in CUTS]
    axes = (("y", "z", "x"), ("z", "x", "y"), ("x", "y", "z"))

    def send(stage, part, k, pick, dst):
        there, device = line_peer(axes[part][stage], k)
        index = (stage * 3 + part) * 3 + k - 1
        copy = pltpu.make_async_remote_copy(
            src_ref=pick(there), dst_ref=dst.at[k - 1],
            send_sem=send_sem.at[index], recv_sem=recv_sem.at[index],
            device_id=device, device_id_type=MESH)
        copy.start()
        return copy

    def add(mine, recv, i):
        total = mine.astype(jnp.float32)
        for k in range(3):
            total = total + recv[(k,) + i].astype(jnp.float32)
        return total

    pending = {}

    def begin():
        picks = (
            lambda t: s_ref.at[:, :, t, :, cols[0]],
            lambda t: s_ref.at[:, t, :, :, cols[1]],
            lambda t: s_ref.at[t, :, :, :, cols[2]],
        )
        pending[0] = [[send(0, p, k, picks[p], (ra0, ra1, ra2)[p]) for k in (2, 1, 3)] for p in range(3)]

    def second():
        pending[1] = []
        for p in range(3):
            for copy in pending[0][p]:
                copy.wait()
            ra, sa = (ra0, ra1, ra2)[p], (sa0, sa1, sa2)[p]

            def step(i, c, p=p, ra=ra, sa=sa):
                a, b = i // 4, lax.rem(i, 4)
                if p == 0:
                    mine = s_ref[a, b, at["y"], :, cols[0]]
                elif p == 1:
                    mine = s_ref[a, at["z"], b, :, cols[1]]
                else:
                    mine = s_ref[at["x"], a, b, :, cols[2]]
                sa[a, b] = add(mine, ra, (a, b)).astype(jnp.bfloat16)
                return c

            lax.fori_loop(0, 16, step, 0)
            pick = (lambda t: sa0.at[:, t], lambda t: sa1.at[t], lambda t: sa2.at[:, t])[p]
            pending[1].append([send(1, p, k, pick, (rb0, rb1, rb2)[p]) for k in (2, 1, 3)])

    def third():
        pending[2] = []
        for p in range(3):
            for copy in pending[1][p]:
                copy.wait()
            rb, sb = (rb0, rb1, rb2)[p], (sb0, sb1, sb2)[p]
            for i in range(4):
                mine = (lambda: sa0[i, at["z"]], lambda: sa1[at["x"], i], lambda: sa2[i, at["y"]])[p]()
                sb[i] = add(mine, rb, (i,)).astype(jnp.bfloat16)
            pending[2].append([send(2, p, k, lambda t, sb=sb: sb.at[t], (rc0, rc1, rc2)[p]) for k in (2, 1, 3)])

    def end():
        for p in range(3):
            for copy in pending[2][p]:
                copy.wait()
            sb, rc = (sb0, sb1, sb2)[p], (rc0, rc1, rc2)[p]
            out_ref[:, cols[p]] = add(sb[at[axes[p][2]]], rc, ())

    return begin, second, third, end


def scan_steps(backward, s_ref, dec_ref, out_ref, got_dec, scratch):
    got, pre, send_a, recv_a, send_d, recv_d, send_b, recv_b, own_sem = scratch
    me = lax.axis_index("ctx")

    def peer_of(k):
        return lax.rem(me + k, N_CTX)

    def state_copy(src, dst, send, recv, strand_at):
        rows = pl.ds(P_SIZE * strand_at, P_SIZE)

        def make(k):
            return pltpu.make_async_remote_copy(
                src_ref=src.at[peer_of(k), rows], dst_ref=dst.at[me, rows],
                send_sem=send.at[strand_at, k], recv_sem=recv.at[strand_at, k],
                device_id={"ctx": peer_of(k)}, device_id_type=MESH)
        return make

    def copy_d(k):
        return pltpu.make_async_remote_copy(
            src_ref=dec_ref.at[peer_of(k)], dst_ref=got_dec.at[me], send_sem=send_d.at[k], recv_sem=recv_d.at[k],
            device_id={"ctx": peer_of(k)}, device_id_type=MESH)

    copy_a = [state_copy(s_ref, got, send_a, recv_a, i) for i in range(2)]
    copy_b = [state_copy(pre, out_ref, send_b, recv_b, i) for i in range(2)]

    def start(make):
        def step(k, c):
            make(k).start()
            return c
        lax.fori_loop(1, N_CTX, step, 0)

    def finish(make):
        def step(k, c):
            make(k).wait()
            return c
        lax.fori_loop(1, N_CTX, step, 0)

    def begin():
        if not backward:
            start(copy_d)
        for i in range(2):
            start(copy_a[i])
        own = pltpu.make_async_copy(s_ref.at[me], got.at[me], own_sem.at[0])
        own.start()
        own.wait()
        if not backward:
            own_d = pltpu.make_async_copy(dec_ref.at[me], got_dec.at[me], own_sem.at[1])
            own_d.start()
            own_d.wait()

    def turn():
        if not backward:
            finish(copy_d)
        decays = dec_ref if backward else got_dec
        for i in range(2):
            finish(copy_a[i])
            rows = slice(P_SIZE * i, P_SIZE * i + P_SIZE)

            def fold(n, carry, i=i, rows=rows):
                at = N_CTX - 1 - n if backward else n
                pre[at, rows, :] = carry.astype(jnp.bfloat16)
                return decays[at, 8 * i : 8 * i + 1, :] * carry + got[at, rows, :].astype(jnp.float32)

            lax.fori_loop(0, N_CTX, fold, jnp.zeros((P_SIZE, NS), jnp.float32))
            start(copy_b[i])

    def end():
        own = pltpu.make_async_copy(pre.at[me], out_ref.at[me], own_sem.at[2])
        own.start()
        own.wait()
        for i in range(2):
            finish(copy_b[i])

    return begin, turn, end


def greet_line():
    me = lax.axis_index("ctx")
    barrier = pltpu.get_barrier_semaphore()

    def step(k, c):
        pl.semaphore_signal(barrier, inc=1, device_id={"ctx": lax.rem(me + k, N_CTX)}, device_id_type=MESH)
        return c

    lax.fori_loop(1, N_CTX, step, 0)
    pl.semaphore_wait(barrier, N_CTX - 1)


def forward_exchange(s_ref, dec_ref, out_ref, got_dec, *scratch):
    begin, turn, end = scan_steps(False, s_ref, dec_ref, out_ref, got_dec, scratch)
    greet_line()
    begin()
    turn()
    end()


def backward_exchange(s_ref, dec_ref, grads, grads_other, normed, normed_other, out_ref, partial, *scratch):
    begin, turn, end = scan_steps(True, s_ref, dec_ref, out_ref, None, scratch)
    greet_line()
    begin()

    def rows(i, c):
        at = pl.ds(pl.multiple_of(i * 256, 128), 256)
        total = dot(grads[:, at], normed[...], ROWS) + dot(grads_other[:, at], normed_other[...], ROWS)
        partial[i] = total.astype(jnp.bfloat16).reshape(4, 4, 16, 2048)
        return c

    lax.fori_loop(0, 4, rows, 0)
    turn()
    end()


def last_exchange(v_ref, weight, out_v, d_weight, plane, line, part, send_a, recv_a, send_b, recv_b, *scratch):
    w_begin, w_second, w_third, w_end = scatter_steps(weight, d_weight, scratch)
    dp, ctx = lax.axis_index("dp"), lax.axis_index("ctx")
    q, x_hi = lax.rem(ctx, 16), ctx // 16
    e = x_hi * 4 + dp

    def peer_a(k):
        return (dp, x_hi * 16 + lax.rem(q + k, 16))

    def peer_b(k):
        there = lax.rem(e + k, 8)
        return (lax.rem(there, 4), (there // 4) * 16 + q)

    barrier = pltpu.get_barrier_semaphore()
    peers = [peer_a(k) for k in range(1, 16)] + [peer_b(k) for k in range(1, 8)]
    peers += [line_peer(axis, k)[1] for axis in "xyz" for k in (1, 2, 3)]
    for device in peers:
        pl.semaphore_signal(barrier, inc=1, device_id=device, device_id_type=MESH)
    pl.semaphore_wait(barrier, len(peers))

    def copy_a(k):
        return pltpu.make_async_remote_copy(
            src_ref=v_ref, dst_ref=plane.at[q], send_sem=send_a.at[k], recv_sem=recv_a.at[k],
            device_id=peer_a(k), device_id_type=MESH)

    def copy_b(k):
        return pltpu.make_async_remote_copy(
            src_ref=part, dst_ref=line.at[e], send_sem=send_b.at[k], recv_sem=recv_b.at[k],
            device_id=peer_b(k), device_id_type=MESH)

    first = [copy_a(k) for k in range(1, 16)]
    for copy in first:
        copy.start()
    w_begin()
    plane[q] = v_ref[...]
    for copy in first:
        copy.wait()
    total = plane[0]
    for i in range(1, 16):
        total = total + plane[i]
    part[...] = total
    line[e] = total
    second = [copy_b(k) for k in range(1, 8)]
    for copy in second:
        copy.start()
    w_second()
    for copy in second:
        copy.wait()
    total = line[0]
    for i in range(1, 8):
        total = total + line[i]
    out_v[...] = total
    w_third()
    w_end()


def exchange_call(kernel, name, collective_id, out_shape, scratch, *args):
    vmem = pl.BlockSpec(memory_space=pltpu.VMEM)
    return pl.pallas_call(
        kernel, out_shape=out_shape, in_specs=[vmem] * len(args), out_specs=[vmem] * len(out_shape),
        scratch_shapes=scratch, name=name,
        compiler_params=pltpu.CompilerParams(collective_id=collective_id, has_side_effects=True),
        cost_estimate=pl.CostEstimate(flops=1000000, bytes_accessed=4000000, transcendentals=0))(*args)


def scan_scratch():
    dma = pltpu.SemaphoreType.DMA
    state = pltpu.VMEM((N_CTX, 128, 128), jnp.bfloat16)
    pairs, singles = dma((2, N_CTX)), dma((N_CTX,))
    return [state, state, pairs, pairs, singles, singles, pairs, pairs, dma((3,))]


def sum_scratch(shape):
    dma = pltpu.SemaphoreType.DMA
    return [
        pltpu.VMEM((16,) + shape, jnp.float32), pltpu.VMEM((8,) + shape, jnp.float32),
        pltpu.VMEM(shape, jnp.float32), dma((16,)), dma((16,)), dma((8,)), dma((8,))]


def scatter_scratch():
    widths = [b - a for a, b in CUTS]
    shapes = ((3, 4, 4, 16), (4, 4, 16), (3, 4, 16), (4, 16), (3, 16))
    scratch = [pltpu.VMEM(shape + (w,), jnp.bfloat16) for shape in shapes for w in widths]
    return scratch + [pltpu.SemaphoreType.DMA((27,)), pltpu.SemaphoreType.DMA((27,))]


H = 32
P_SIZE = 64
NS = 128
DI = 2048
Q = 128
PAIRS = 16
B_AT = 2 * DI
C_AT = 2 * DI + NS
bf16 = jnp.bfloat16
f32 = jnp.float32
precise = lax.Precision.HIGHEST


def dot(a, b, dims=((1,), (0,)), precision=None):
    return lax.dot_general(a, b, (dims, ((), ())), precision=precision, preferred_element_type=f32)


ROWS = ((0,), (0,))
LANES = ((1,), (1,))


def iota(shape, axis):
    return lax.broadcasted_iota(jnp.int32, shape, axis)


def head_map():
    return (iota((H, DI), 0) == iota((H, DI), 1) // P_SIZE).astype(f32).astype(bf16)


def expand(value, heads):
    high = value.astype(bf16)
    low = (value - high.astype(f32)).astype(bf16)
    return dot(high, heads) + dot(low, heads)


def per_head(value, heads):
    return dot(value.astype(bf16), heads, LANES)


def softplus(value):
    return jnp.maximum(value, 0.0) + jnp.log1p(jnp.exp(-jnp.abs(value)))


def sigmoid(value):
    return 1.0 / (1.0 + jnp.exp(-value))


def tril():
    return iota((Q, Q), 0) >= iota((Q, Q), 1)


def half_masks():
    left = (iota((Q, 128), 1) < P_SIZE).astype(f32)
    return left.astype(bf16), (1.0 - left).astype(bf16)


def summary_kernel(proj, dt_raw, a_log, bias, state, decay, dt_out, run_out, dt_t_out, run_t_out):
    lower = tril().astype(f32)
    same = (iota((Q, Q), 0) == iota((Q, Q), 1)).astype(f32)
    dt = softplus(dt_raw[0].astype(f32) + bias[...])
    run = dot(lower, -jnp.exp(a_log[...]) * dt, precision=precise)
    run_t = dot(run, same, ROWS, precision=precise)
    dt_out[0] = dt
    run_out[0] = run
    dt_t_out[0] = dot(dt, same, ROWS, precision=precise)
    run_t_out[0] = run_t
    weight = jnp.exp(run[Q - 1 : Q, :] - run) * dt
    weighed = (expand(weight, head_map()) * proj[0, :, DI:B_AT].astype(f32)).astype(bf16)
    total = dot(weighed, proj[0, :, B_AT:C_AT], ROWS)
    state[...] = total.astype(bf16).reshape(H, P_SIZE, NS)
    left = jnp.exp(run_t[:, Q - 1 : Q])
    for h in range(H):
        decay[h] = jnp.broadcast_to(left[h : h + 1, :], (8, 128))


def forward_kernel(proj, run, dt_t, run_t, entering, skip, gain, normed, y_out, spread_out, mix_out, local):
    write, read = proj[0, :, B_AT:C_AT], proj[0, :, C_AT:]
    affinity = dot(read, write, LANES)
    affinity = jnp.concatenate([affinity, affinity], 1)
    causal = tril()
    left, right = half_masks()
    for j in range(PAIRS):
        cols = slice(DI + 128 * j, DI + 128 * j + 128)
        both = []
        for h in (2 * j, 2 * j + 1):
            gap = run[0, :, h : h + 1] - run_t[0, h : h + 1, :]
            both.append(jnp.exp(jnp.where(causal, gap, -1e30)) * dt_t[0, h : h + 1, :])
        spread = jnp.concatenate(both, 1)
        spread_out[0, j] = spread.astype(bf16)
        values = proj[0, :, cols]
        stacked = jnp.concatenate([values * left, values * right], 0)
        mixing = (spread * affinity).astype(bf16)
        mix_out[0, j] = mixing
        local[:, 128 * j : 128 * j + 128] = dot(mixing, stacked)
    carried = dot(read, entering[...].reshape(DI, NS), LANES)
    grown = expand(jnp.exp(run[0]), head_map())
    y = local[...] + grown * carried + skip[...] * proj[0, :, DI:B_AT].astype(f32)
    y_out[0] = y
    gate = proj[0, :, :DI].astype(f32)
    gated = y * gate * sigmoid(gate)
    inv = lax.rsqrt(jnp.mean(gated * gated, axis=1, keepdims=True) + 1e-05)
    normed[0] = (gated * inv * gain[...]).astype(bf16)


def backward_kernel(proj, y_in, d_normed, run, spread_in, mix_in, entering, skip, gain,
                    d_gate, d_x, d_entering, d_write, d_read, gains, from_y, from_x, dy_keep, dx_keep):
    heads = head_map()
    gate = proj[0, :, :DI].astype(f32)
    y = y_in[0]
    sig = sigmoid(gate)
    silu = gate * sig
    gated = y * silu
    inv = lax.rsqrt(jnp.mean(gated * gated, axis=1, keepdims=True) + 1e-05)
    dn = d_normed[0].astype(f32)
    gains[0, 0:1, :] = jnp.sum(dn * (gated * inv), axis=0, keepdims=True)
    up = dn * gain[...]
    pull = jnp.mean(up * gated, axis=1, keepdims=True) * (inv * inv * inv)
    d_gated = inv * up - gated * pull
    dy = d_gated * silu
    d_gate[0] = (d_gated * y * (sig * (1.0 + gate * (1.0 - sig)))).astype(bf16)
    values = proj[0, :, DI:B_AT].astype(f32)
    gains[0, 1:2, :] = jnp.sum(dy * values, axis=0, keepdims=True)
    dy_keep[...] = dy.astype(bf16)
    from_y[0] = per_head(dy_keep[...].astype(f32) * (y - skip[...] * values), heads)
    grown = (expand(jnp.exp(run[0]), heads) * dy).astype(bf16)
    write, read = proj[0, :, B_AT:C_AT], proj[0, :, C_AT:]
    state = entering[...].reshape(DI, NS)
    d_entering[...] = dot(grown, read, ROWS).astype(bf16).reshape(H, P_SIZE, NS)
    d_c = dot(grown, state)
    left, right = half_masks()
    first = iota((Q, 128), 1) < P_SIZE
    d_aff = jnp.zeros((Q, Q), f32)
    for j in range(PAIRS):
        cols = slice(128 * j, 128 * j + 128)
        dyp = dy_keep[:, cols]
        x = proj[0, :, DI + 128 * j : DI + 128 * j + 128]
        stacked = jnp.concatenate([x * left, x * right], 0)
        d_mix = dot(dyp, stacked, LANES) * spread_in[0, j].astype(f32)
        d_aff = d_aff + d_mix[:, :Q] + d_mix[:, Q:]
        back = dot(mix_in[0, j], dyp, ROWS)
        dx_keep[:, cols] = jnp.where(first, back[:Q], back[Q:])
    d_aff = d_aff.astype(bf16)
    d_read[0] = (d_c + dot(d_aff, write)).astype(bf16)
    d_write[0] = dot(d_aff, read, ROWS)
    dx = dx_keep[...]
    from_x[0] = per_head(values * dx, heads)
    d_x[0] = dx + skip[...] * dy


def finish_kernel(proj, dt_raw, dt_in, run_in, leaving, entering, from_y, from_x, d_x, d_gate, d_write, d_read,
                  a_log, bias, d_proj, d_dt, sums):
    heads = head_map()
    rate = jnp.exp(a_log[...])
    dt, run = dt_in[0], run_in[0]
    last = run[Q - 1 : Q, :]
    weight = expand(jnp.exp(last - run) * dt, heads)
    values = proj[0, :, DI:B_AT].astype(f32)
    out = leaving[...].reshape(DI, NS)
    d_state = weight * dot(proj[0, :, B_AT:C_AT], out, LANES)
    d_b = d_write[0] + dot((weight * values).astype(bf16), out)
    d_proj[0, :, :DI] = d_gate[0]
    d_proj[0, :, DI:B_AT] = (d_x[0] + d_state).astype(bf16)
    d_proj[0, :, B_AT:C_AT] = d_b.astype(bf16)
    d_proj[0, :, C_AT:] = d_read[0]
    from_state = per_head(values * d_state, heads)
    total = from_x[0] + from_state
    meet = jnp.sum(entering[...].astype(f32) * leaving[...].astype(f32), axis=1)
    meet = dot(jnp.ones((8, NS), f32), meet, LANES, precision=precise)[0:1, :]
    d_last = jnp.exp(last) * meet + jnp.sum(from_state, axis=0, keepdims=True)
    upper = (iota((Q, Q), 0) <= iota((Q, Q), 1)).astype(f32)
    d_log = dot(upper, from_y[0] - total, precision=precise) + d_last
    d_step = total / dt - rate * d_log
    d_raw = d_step * sigmoid(dt_raw[0].astype(f32) + bias[...])
    d_dt[0] = d_raw.astype(bf16)
    sums[0, 0:1, :] = jnp.sum(d_log * (-rate * dt), axis=0, keepdims=True)
    sums[0, 1:2, :] = jnp.sum(d_raw, axis=0, keepdims=True)


def strand(*shape):
    return pl.BlockSpec((1,) + shape, lambda s: (s,) + (0,) * len(shape))


def shared(*shape):
    return pl.BlockSpec(shape, lambda s: (0,) * len(shape))


STATE = pl.BlockSpec((H, P_SIZE, NS), lambda s: (0, s, 0))


def like(dtype, *shape):
    return jax.ShapeDtypeStruct(shape, dtype)


def strand_call(kernel, name, in_specs, out_specs, out_shape, scratch=(), flops=2000000000):
    return pl.pallas_call(
        kernel, grid=(2,), in_specs=in_specs, out_specs=out_specs, out_shape=out_shape,
        scratch_shapes=list(scratch), name=name,
        cost_estimate=pl.CostEstimate(flops=flops, bytes_accessed=10000000, transcendentals=0))


def flipped(block):
    turn = (iota((128, 128), 0) + iota((128, 128), 1) == 127).astype(f32).astype(bf16)
    rows = dot(turn, block).astype(bf16)
    parts = [dot(rows[:, 128 * j : 128 * j + 128], turn) for j in range(15, -1, -1)]
    return jnp.concatenate(parts, 1)


def flip_kernel(keep, got, out, mine, theirs):
    out[0] = keep[...]
    out[1] = flipped(got[...]).astype(bf16)
    core = lax.rem(lax.axis_index("dp"), 2)
    for s in range(2):
        for half in range(2):
            rows, cols = slice(Q * s, Q * s + Q), slice(512 * half, 512 * half + 512)
            mine[rows, cols] = out[s, :, pl.ds(pl.multiple_of((2 * half + core) * 512, 128), 512)]
            theirs[rows, cols] = out[s, :, pl.ds(pl.multiple_of((2 * half + 1 - core) * 512, 128), 512)]


def mix_kernel(own, got, out):
    out[...] = (own[...].astype(f32) + flipped(got[...])).astype(bf16)


def whole_call(kernel, name, out_shape, *args):
    vmem = pl.BlockSpec(memory_space=pltpu.VMEM)
    return pl.pallas_call(
        kernel, out_shape=out_shape, in_specs=[vmem] * len(args), out_specs=jax.tree.map(lambda _: vmem, out_shape), name=name,
        cost_estimate=pl.CostEstimate(flops=200000000, bytes_accessed=2000000, transcendentals=0))(*args)


def mirror(value):
    return lax.ppermute(value, "ctx", [(i, N_CTX - 1 - i) for i in range(N_CTX)])


def other_core(value):
    return lax.ppermute(value, "dp", [(i, i ^ 1) for i in range(4)])


def body(projections, dt_raw, a_log, dt_bias, skip_gain, norm_gain, w_out, base_ids, cotangent):
    keep = cotangent * (base_ids != 4).astype(bf16)[:, None]
    got_keep = mirror(keep)
    proj, tok = strand(Q, 2 * DI + 2 * NS), strand(Q, H)
    tok_t, wide = strand(H, Q), strand(Q, DI)
    row, lane = shared(1, H), shared(1, DI)
    skip, gain = jnp.repeat(skip_gain, P_SIZE)[None], norm_gain[None]
    state, factor, dt, run, dt_t, run_t = strand_call(
        summary_kernel, "summary", [proj, tok, row, row],
        [STATE, pl.BlockSpec((H, 8, NS), lambda s: (0, s, 0)), tok, tok, tok_t, tok_t],
        [like(bf16, H, 2 * P_SIZE, NS), like(f32, H, 16, NS), like(f32, 2, Q, H), like(f32, 2, Q, H),
         like(f32, 2, H, Q), like(f32, 2, H, Q)],
    )(projections, dt_raw, a_log[None], dt_bias[None])
    states = like(bf16, H, 2 * P_SIZE, NS)
    entering, decays = exchange_call(
        forward_exchange, "forward_exchange", 1, [states, like(f32, H, 16, NS)], scan_scratch(), state, factor)
    d_out, grads, grads_away = whole_call(
        flip_kernel, "flip_keep", [like(bf16, 2, Q, DI)] + [like(bf16, 2 * Q, DI // 2)] * 2, keep, got_keep)
    spread_spec = strand(PAIRS, Q, 2 * Q)
    normed, y, spread, mixing = strand_call(
        forward_kernel, "forward", [proj, tok, tok_t, tok_t, STATE, lane, lane],
        [wide, wide, spread_spec, spread_spec],
        [like(bf16, 2, Q, DI), like(f32, 2, Q, DI), like(bf16, 2, PAIRS, Q, 2 * Q),
         like(bf16, 2, PAIRS, Q, 2 * Q)],
        [pltpu.VMEM((Q, DI), f32)],
    )(projections, run, dt_t, run_t, entering, skip, gain)
    strand_out = jnp.einsum("srk,dk->srd", normed, w_out, preferred_element_type=f32).astype(bf16)
    moved = mirror(strand_out[1])
    d_normed = jnp.einsum("srd,dk->srk", d_out, w_out, preferred_element_type=f32).astype(bf16)
    d_gate, d_x, d_entering, d_write, d_read, gains, from_y, from_x = strand_call(
        backward_kernel, "backward", [proj, wide, wide, tok, spread_spec, spread_spec, STATE, lane, lane],
        [wide, wide, STATE, strand(Q, NS), strand(Q, NS), strand(2, DI), tok, tok],
        [like(bf16, 2, Q, DI), like(f32, 2, Q, DI), like(bf16, H, 2 * P_SIZE, NS), like(f32, 2, Q, NS),
         like(bf16, 2, Q, NS), like(f32, 2, 2, DI), like(f32, 2, Q, H), like(f32, 2, Q, H)],
        [pltpu.VMEM((Q, DI), bf16), pltpu.VMEM((Q, DI), f32)],
    )(projections, y, d_normed, run, spread, mixing, entering, skip, gain)
    flat = normed.reshape(2 * Q, DI)
    leaving, partial = exchange_call(
        backward_exchange, "backward_exchange", 2, [states, like(bf16, 4, 4, 4, 16, DI)], scan_scratch(),
        d_entering, decays, grads, other_core(grads_away), flat, other_core(flat))
    mixed_out = whole_call(mix_kernel, "mix", like(bf16, Q, DI), strand_out[0], moved)
    d_proj, d_dt, sums = strand_call(
        finish_kernel, "finish",
        [proj, tok, tok, tok, STATE, STATE, tok, tok, wide, wide, strand(Q, NS), strand(Q, NS), row, row],
        [proj, tok, strand(2, H)],
        [like(bf16, 2, Q, 2 * DI + 2 * NS), like(bf16, 2, Q, H), like(f32, 2, 2, H)],
    )(projections, dt_raw, dt, run, leaving, entering, from_y, from_x, d_x, d_gate, d_write, d_read,
      a_log[None], dt_bias[None])
    gains = jnp.sum(gains, axis=0)
    d_skip = jnp.sum(gains[1].reshape(H, P_SIZE), axis=1)
    small = jnp.concatenate([gains[0], jnp.sum(sums, axis=0).reshape(-1), d_skip, jnp.zeros((928,), f32)])
    summed, d_w_out = exchange_call(
        last_exchange, "last_exchange", 3, [like(f32, 24, 128), like(f32, 16, DI)],
        sum_scratch((24, 128)) + scatter_scratch(), small.reshape(24, 128), partial)
    summed = summed.reshape(-1)
    return (mixed_out, d_proj, d_dt, d_w_out, summed[2048 : 2048 + 96].reshape(3, 32), summed[:2048])


def solution(mesh):
    placed = (
        P(None, ("dp", "ctx"), None),
        P(None, ("dp", "ctx"), None),
        P(),
        P(),
        P(),
        P(),
        P(),
        P(("dp", "ctx")),
        P(("dp", "ctx"), None),
    )
    return jax.shard_map(
        body,
        mesh=mesh,
        in_specs=placed,
        out_specs=(
            P(("dp", "ctx"), None),
            P(None, ("dp", "ctx"), None),
            P(None, ("dp", "ctx"), None),
            P(("dp", "ctx"), None),
            P(),
            P(),
        ),
        check_vma=False,
    )
```

```python
import functools

import jax
import jax.numpy as jnp
from jax import lax
from jax.experimental import pallas as pl
from jax.experimental.pallas import tpu as pltpu
from jax.sharding import PartitionSpec as P

MESH = pl.DeviceIdType.MESH
N_CTX = 32


CUTS = ((0, 768), (768, 1408), (1408, 2048))


def place():
    dp, ctx = lax.axis_index("dp"), lax.axis_index("ctx")
    x_lo, core = dp // 2, lax.rem(dp, 2)
    x_hi, z, y = ctx // 16, lax.rem(ctx // 4, 4), lax.rem(ctx, 4)
    return dp, core, {"x": x_lo * 2 + x_hi, "z": z, "y": y}


def line_peer(axis, k):
    dp, core, at = place()
    there = lax.rem(at[axis] + k, 4)
    x = there if axis == "x" else at["x"]
    z = there if axis == "z" else at["z"]
    y = there if axis == "y" else at["y"]
    return there, ((x // 2) * 2 + core, lax.rem(x, 2) * 16 + z * 4 + y)


def scatter_steps(s_ref, out_ref, scratch):
    (ra0, ra1, ra2, sa0, sa1, sa2, rb0, rb1, rb2, sb0, sb1, sb2, rc0, rc1, rc2, send_sem, recv_sem) = scratch
    _, _, at = place()
    cols = [pl.ds(a, b - a) for a, b in CUTS]
    axes = (("y", "z", "x"), ("z", "x", "y"), ("x", "y", "z"))

    def send(stage, part, k, pick, dst):
        there, device = line_peer(axes[part][stage], k)
        index = (stage * 3 + part) * 3 + k - 1
        copy = pltpu.make_async_remote_copy(
            src_ref=pick(there), dst_ref=dst.at[k - 1],
            send_sem=send_sem.at[index], recv_sem=recv_sem.at[index],
            device_id=device, device_id_type=MESH)
        copy.start()
        return copy

    def add(mine, recv, i):
        total = mine.astype(jnp.float32)
        for k in range(3):
            total = total + recv[(k,) + i].astype(jnp.float32)
        return total

    pending = {}

    def begin():
        picks = (
            lambda t: s_ref.at[:, :, t, :, cols[0]],
            lambda t: s_ref.at[:, t, :, :, cols[1]],
            lambda t: s_ref.at[t, :, :, :, cols[2]],
        )
        pending[0] = [[send(0, p, k, picks[p], (ra0, ra1, ra2)[p]) for k in (2, 1, 3)] for p in range(3)]

    def second():
        pending[1] = []
        for p in range(3):
            for copy in pending[0][p]:
                copy.wait()
            ra, sa = (ra0, ra1, ra2)[p], (sa0, sa1, sa2)[p]

            def step(i, c, p=p, ra=ra, sa=sa):
                a, b = i // 4, lax.rem(i, 4)
                if p == 0:
                    mine = s_ref[a, b, at["y"], :, cols[0]]
                elif p == 1:
                    mine = s_ref[a, at["z"], b, :, cols[1]]
                else:
                    mine = s_ref[at["x"], a, b, :, cols[2]]
                sa[a, b] = add(mine, ra, (a, b)).astype(jnp.bfloat16)
                return c

            lax.fori_loop(0, 16, step, 0)
            pick = (lambda t: sa0.at[:, t], lambda t: sa1.at[t], lambda t: sa2.at[:, t])[p]
            pending[1].append([send(1, p, k, pick, (rb0, rb1, rb2)[p]) for k in (2, 1, 3)])

    def third():
        pending[2] = []
        for p in range(3):
            for copy in pending[1][p]:
                copy.wait()
            rb, sb = (rb0, rb1, rb2)[p], (sb0, sb1, sb2)[p]
            for i in range(4):
                mine = (lambda: sa0[i, at["z"]], lambda: sa1[at["x"], i], lambda: sa2[i, at["y"]])[p]()
                sb[i] = add(mine, rb, (i,)).astype(jnp.bfloat16)
            pending[2].append([send(2, p, k, lambda t, sb=sb: sb.at[t], (rc0, rc1, rc2)[p]) for k in (2, 1, 3)])

    def end():
        for p in range(3):
            for copy in pending[2][p]:
                copy.wait()
            sb, rc = (sb0, sb1, sb2)[p], (rc0, rc1, rc2)[p]
            out_ref[:, cols[p]] = add(sb[at[axes[p][2]]], rc, ())

    return begin, second, third, end


def scan_steps(backward, s_ref, dec_ref, out_ref, got_dec, scratch):
    got, pre, send_a, recv_a, send_d, recv_d, send_b, recv_b, own_sem = scratch
    me = lax.axis_index("ctx")

    def peer_of(k):
        return lax.rem(me + k * 5, N_CTX)

    def state_copy(src, dst, send, recv, strand_at):
        rows = pl.ds(P_SIZE * strand_at, P_SIZE)

        def make(k):
            return pltpu.make_async_remote_copy(
                src_ref=src.at[peer_of(k), rows], dst_ref=dst.at[me, rows],
                send_sem=send.at[strand_at, k], recv_sem=recv.at[strand_at, k],
                device_id={"ctx": peer_of(k)}, device_id_type=MESH)
        return make

    def copy_d(k):
        return pltpu.make_async_remote_copy(
            src_ref=dec_ref.at[peer_of(k)], dst_ref=got_dec.at[me], send_sem=send_d.at[k], recv_sem=recv_d.at[k],
            device_id={"ctx": peer_of(k)}, device_id_type=MESH)

    copy_a = [state_copy(s_ref, got, send_a, recv_a, i) for i in range(2)]
    copy_b = [state_copy(pre, out_ref, send_b, recv_b, i) for i in range(2)]

    def start(make):
        def step(k, c):
            make(k).start()
            return c
        lax.fori_loop(1, N_CTX, step, 0)

    def finish(make):
        def step(k, c):
            make(k).wait()
            return c
        lax.fori_loop(1, N_CTX, step, 0)

    def begin():
        if not backward:
            start(copy_d)
        for i in range(2):
            start(copy_a[i])
        own = pltpu.make_async_copy(s_ref.at[me], got.at[me], own_sem.at[0])
        own.start()
        own.wait()
        if not backward:
            own_d = pltpu.make_async_copy(dec_ref.at[me], got_dec.at[me], own_sem.at[1])
            own_d.start()
            own_d.wait()

    def turn():
        if not backward:
            finish(copy_d)
        decays = dec_ref if backward else got_dec
        for i in range(2):
            finish(copy_a[i])
            rows = slice(P_SIZE * i, P_SIZE * i + P_SIZE)

            def fold(n, carry, i=i, rows=rows):
                at = N_CTX - 1 - n if backward else n
                pre[at, rows, :] = carry.astype(jnp.bfloat16)
                return decays[at, 8 * i : 8 * i + 1, :] * carry + got[at, rows, :].astype(jnp.float32)

            lax.fori_loop(0, N_CTX, fold, jnp.zeros((P_SIZE, NS), jnp.float32))
            start(copy_b[i])

    def end():
        own = pltpu.make_async_copy(pre.at[me], out_ref.at[me], own_sem.at[2])
        own.start()
        own.wait()
        for i in range(2):
            finish(copy_b[i])

    return begin, turn, end


def greet_line():
    me = lax.axis_index("ctx")
    barrier = pltpu.get_barrier_semaphore()

    def step(k, c):
        pl.semaphore_signal(barrier, inc=1, device_id={"ctx": lax.rem(me + k, N_CTX)}, device_id_type=MESH)
        return c

    lax.fori_loop(1, N_CTX, step, 0)
    pl.semaphore_wait(barrier, N_CTX - 1)


def forward_exchange(s_ref, dec_ref, proj, run, dt_t, run_t, out_ref, got_dec, local, spread_out, mix_out, *scratch):
    begin, turn, end = scan_steps(False, s_ref, dec_ref, out_ref, got_dec, scratch)
    greet_line()
    begin()

    def block(s, c):
        local_outputs(s, proj, run, dt_t, run_t, local, spread_out, mix_out)
        return c

    lax.fori_loop(0, 2, block, 0)
    turn()
    end()


def backward_exchange(s_ref, dec_ref, grads, grads_other, normed, normed_other, out_ref, partial, *scratch):
    begin, turn, end = scan_steps(True, s_ref, dec_ref, out_ref, None, scratch)
    greet_line()
    begin()

    def rows(i, c):
        at = pl.ds(pl.multiple_of(i * 256, 128), 256)
        total = dot(grads[:, at], normed[...], ROWS) + dot(grads_other[:, at], normed_other[...], ROWS)
        partial[i] = total.astype(jnp.bfloat16).reshape(4, 4, 16, 2048)
        return c

    lax.fori_loop(0, 4, rows, 0)
    turn()
    end()


def last_exchange(v_ref, weight, out_v, d_weight, plane, line, part, send_a, recv_a, send_b, recv_b, *scratch):
    w_begin, w_second, w_third, w_end = scatter_steps(weight, d_weight, scratch)
    dp, ctx = lax.axis_index("dp"), lax.axis_index("ctx")
    q, x_hi = lax.rem(ctx, 16), ctx // 16
    e = x_hi * 4 + dp

    def peer_a(k):
        return (dp, x_hi * 16 + lax.rem(q + k, 16))

    def peer_b(k):
        there = lax.rem(e + k, 8)
        return (lax.rem(there, 4), (there // 4) * 16 + q)

    barrier = pltpu.get_barrier_semaphore()
    peers = [peer_a(k) for k in range(1, 16)] + [peer_b(k) for k in range(1, 8)]
    peers += [line_peer(axis, k)[1] for axis in "xyz" for k in (1, 2, 3)]
    for device in peers:
        pl.semaphore_signal(barrier, inc=1, device_id=device, device_id_type=MESH)
    pl.semaphore_wait(barrier, len(peers))

    def copy_a(k):
        return pltpu.make_async_remote_copy(
            src_ref=v_ref, dst_ref=plane.at[q], send_sem=send_a.at[k], recv_sem=recv_a.at[k],
            device_id=peer_a(k), device_id_type=MESH)

    def copy_b(k):
        return pltpu.make_async_remote_copy(
            src_ref=part, dst_ref=line.at[e], send_sem=send_b.at[k], recv_sem=recv_b.at[k],
            device_id=peer_b(k), device_id_type=MESH)

    first = [copy_a(k) for k in range(1, 16)]
    for copy in first:
        copy.start()
    w_begin()
    plane[q] = v_ref[...]
    for copy in first:
        copy.wait()
    total = plane[0]
    for i in range(1, 16):
        total = total + plane[i]
    part[...] = total
    line[e] = total
    second = [copy_b(k) for k in range(1, 8)]
    for copy in second:
        copy.start()
    w_second()
    for copy in second:
        copy.wait()
    total = line[0]
    for i in range(1, 8):
        total = total + line[i]
    out_v[...] = total
    w_third()
    w_end()


def exchange_call(kernel, name, collective_id, out_shape, scratch, *args):
    vmem = pl.BlockSpec(memory_space=pltpu.VMEM)
    return pl.pallas_call(
        kernel, out_shape=out_shape, in_specs=[vmem] * len(args), out_specs=[vmem] * len(out_shape),
        scratch_shapes=scratch, name=name,
        compiler_params=pltpu.CompilerParams(collective_id=collective_id, has_side_effects=True),
        cost_estimate=pl.CostEstimate(flops=1000000, bytes_accessed=4000000, transcendentals=0))(*args)


def scan_scratch():
    dma = pltpu.SemaphoreType.DMA
    state = pltpu.VMEM((N_CTX, 128, 128), jnp.bfloat16)
    pairs, singles = dma((2, N_CTX)), dma((N_CTX,))
    return [state, state, pairs, pairs, singles, singles, pairs, pairs, dma((3,))]


def sum_scratch(shape):
    dma = pltpu.SemaphoreType.DMA
    return [
        pltpu.VMEM((16,) + shape, jnp.float32), pltpu.VMEM((8,) + shape, jnp.float32),
        pltpu.VMEM(shape, jnp.float32), dma((16,)), dma((16,)), dma((8,)), dma((8,))]


def scatter_scratch():
    widths = [b - a for a, b in CUTS]
    shapes = ((3, 4, 4, 16), (4, 4, 16), (3, 4, 16), (4, 16), (3, 16))
    scratch = [pltpu.VMEM(shape + (w,), jnp.bfloat16) for shape in shapes for w in widths]
    return scratch + [pltpu.SemaphoreType.DMA((27,)), pltpu.SemaphoreType.DMA((27,))]


H = 32
P_SIZE = 64
NS = 128
DI = 2048
Q = 128
PAIRS = 16
B_AT = 2 * DI
C_AT = 2 * DI + NS
bf16 = jnp.bfloat16
f32 = jnp.float32
precise = lax.Precision.HIGHEST


def dot(a, b, dims=((1,), (0,)), precision=None):
    return lax.dot_general(a, b, (dims, ((), ())), precision=precision, preferred_element_type=f32)


ROWS = ((0,), (0,))
LANES = ((1,), (1,))


def iota(shape, axis):
    return lax.broadcasted_iota(jnp.int32, shape, axis)


def head_map():
    return (iota((H, DI), 0) == iota((H, DI), 1) // P_SIZE).astype(f32).astype(bf16)


def expand(value, heads):
    high = value.astype(bf16)
    low = (value - high.astype(f32)).astype(bf16)
    return dot(high, heads) + dot(low, heads)


def per_head(value, heads):
    return dot(value.astype(bf16), heads, LANES)


def softplus(value):
    return jnp.maximum(value, 0.0) + jnp.log1p(jnp.exp(-jnp.abs(value)))


def sigmoid(value):
    return 1.0 / (1.0 + jnp.exp(-value))


def tril():
    return iota((Q, Q), 0) >= iota((Q, Q), 1)


def half_masks():
    left = (iota((Q, 128), 1) < P_SIZE).astype(f32)
    return left.astype(bf16), (1.0 - left).astype(bf16)


def summary_kernel(proj, dt_raw, a_log, bias, state, decay, dt_out, run_out, dt_t_out, run_t_out):
    lower = tril().astype(f32)
    same = (iota((Q, Q), 0) == iota((Q, Q), 1)).astype(f32)
    dt = softplus(dt_raw[0].astype(f32) + bias[...])
    run = dot(lower, -jnp.exp(a_log[...]) * dt, precision=precise)
    run_t = dot(run, same, ROWS, precision=precise)
    dt_out[0] = dt
    run_out[0] = run
    dt_t_out[0] = dot(dt, same, ROWS, precision=precise)
    run_t_out[0] = run_t
    weight = jnp.exp(run[Q - 1 : Q, :] - run) * dt
    weighed = (expand(weight, head_map()) * proj[0, :, DI:B_AT].astype(f32)).astype(bf16)
    total = dot(weighed, proj[0, :, B_AT:C_AT], ROWS)
    state[...] = total.astype(bf16).reshape(H, P_SIZE, NS)
    left = jnp.exp(run_t[:, Q - 1 : Q])
    for h in range(H):
        decay[h] = jnp.broadcast_to(left[h : h + 1, :], (8, 128))


def local_outputs(s, proj, run, dt_t, run_t, local, spread_out, mix_out):
    affinity = dot(proj[s, :, C_AT:], proj[s, :, B_AT:C_AT], LANES)
    affinity = jnp.concatenate([affinity, affinity], 1)
    causal = tril()
    left, right = half_masks()
    for j in range(PAIRS):
        cols = slice(DI + 128 * j, DI + 128 * j + 128)
        both = []
        for h in (2 * j, 2 * j + 1):
            gap = run[s, :, h : h + 1] - run_t[s, h : h + 1, :]
            both.append(jnp.exp(jnp.where(causal, gap, -1e30)) * dt_t[s, h : h + 1, :])
        spread = jnp.concatenate(both, 1)
        spread_out[s, j] = spread.astype(bf16)
        values = proj[s, :, cols]
        stacked = jnp.concatenate([values * left, values * right], 0)
        mixing = (spread * affinity).astype(bf16)
        mix_out[s, j] = mixing
        local[s, :, 128 * j : 128 * j + 128] = dot(mixing, stacked)


def forward_kernel(proj, run, local, entering, skip, gain, normed, y_out):
    carried = dot(proj[0, :, C_AT:], entering[...].reshape(DI, NS), LANES)
    grown = expand(jnp.exp(run[0]), head_map())
    y = local[0] + grown * carried + skip[...] * proj[0, :, DI:B_AT].astype(f32)
    y_out[0] = y
    gate = proj[0, :, :DI].astype(f32)
    gated = y * gate * sigmoid(gate)
    inv = lax.rsqrt(jnp.mean(gated * gated, axis=1, keepdims=True) + 1e-05)
    normed[0] = (gated * inv * gain[...]).astype(bf16)


def backward_kernel(proj, y_in, d_normed, run, spread_in, mix_in, entering, skip, gain,
                    d_gate, d_x, d_entering, d_write, d_read, gains, from_y, from_x, dy_keep, dx_keep):
    heads = head_map()
    gate = proj[0, :, :DI].astype(f32)
    y = y_in[0]
    sig = sigmoid(gate)
    silu = gate * sig
    gated = y * silu
    inv = lax.rsqrt(jnp.mean(gated * gated, axis=1, keepdims=True) + 1e-05)
    dn = d_normed[0].astype(f32)
    gains[0, 0:1, :] = jnp.sum(dn * (gated * inv), axis=0, keepdims=True)
    up = dn * gain[...]
    pull = jnp.mean(up * gated, axis=1, keepdims=True) * (inv * inv * inv)
    d_gated = inv * up - gated * pull
    dy = d_gated * silu
    d_gate[0] = (d_gated * y * (sig * (1.0 + gate * (1.0 - sig)))).astype(bf16)
    values = proj[0, :, DI:B_AT].astype(f32)
    gains[0, 1:2, :] = jnp.sum(dy * values, axis=0, keepdims=True)
    dy_keep[...] = dy.astype(bf16)
    from_y[0] = per_head(dy_keep[...].astype(f32) * (y - skip[...] * values), heads)
    grown = (expand(jnp.exp(run[0]), heads) * dy).astype(bf16)
    write, read = proj[0, :, B_AT:C_AT], proj[0, :, C_AT:]
    state = entering[...].reshape(DI, NS)
    d_entering[...] = dot(grown, read, ROWS).astype(bf16).reshape(H, P_SIZE, NS)
    d_c = dot(grown, state)
    left, right = half_masks()
    first = iota((Q, 128), 1) < P_SIZE
    d_aff = jnp.zeros((Q, Q), f32)
    for j in range(PAIRS):
        cols = slice(128 * j, 128 * j + 128)
        dyp = dy_keep[:, cols]
        x = proj[0, :, DI + 128 * j : DI + 128 * j + 128]
        stacked = jnp.concatenate([x * left, x * right], 0)
        d_mix = dot(dyp, stacked, LANES) * spread_in[0, j].astype(f32)
        d_aff = d_aff + d_mix[:, :Q] + d_mix[:, Q:]
        back = dot(mix_in[0, j], dyp, ROWS)
        dx_keep[:, cols] = jnp.where(first, back[:Q], back[Q:])
    d_aff = d_aff.astype(bf16)
    d_read[0] = (d_c + dot(d_aff, write)).astype(bf16)
    d_write[0] = dot(d_aff, read, ROWS)
    dx = dx_keep[...]
    from_x[0] = per_head(values * dx, heads)
    d_x[0] = dx + skip[...] * dy


def finish_kernel(proj, dt_raw, dt_in, run_in, leaving, entering, from_y, from_x, d_x, d_gate, d_write, d_read,
                  a_log, bias, d_proj, d_dt, sums):
    heads = head_map()
    rate = jnp.exp(a_log[...])
    dt, run = dt_in[0], run_in[0]
    last = run[Q - 1 : Q, :]
    weight = expand(jnp.exp(last - run) * dt, heads)
    values = proj[0, :, DI:B_AT].astype(f32)
    out = leaving[...].reshape(DI, NS)
    d_state = weight * dot(proj[0, :, B_AT:C_AT], out, LANES)
    d_b = d_write[0] + dot((weight * values).astype(bf16), out)
    d_proj[0, :, :DI] = d_gate[0]
    d_proj[0, :, DI:B_AT] = (d_x[0] + d_state).astype(bf16)
    d_proj[0, :, B_AT:C_AT] = d_b.astype(bf16)
    d_proj[0, :, C_AT:] = d_read[0]
    from_state = per_head(values * d_state, heads)
    total = from_x[0] + from_state
    meet = jnp.sum(entering[...].astype(f32) * leaving[...].astype(f32), axis=1)
    meet = dot(jnp.ones((8, NS), f32), meet, LANES, precision=precise)[0:1, :]
    d_last = jnp.exp(last) * meet + jnp.sum(from_state, axis=0, keepdims=True)
    upper = (iota((Q, Q), 0) <= iota((Q, Q), 1)).astype(f32)
    d_log = dot(upper, from_y[0] - total, precision=precise) + d_last
    d_step = total / dt - rate * d_log
    d_raw = d_step * sigmoid(dt_raw[0].astype(f32) + bias[...])
    d_dt[0] = d_raw.astype(bf16)
    sums[0, 0:1, :] = jnp.sum(d_log * (-rate * dt), axis=0, keepdims=True)
    sums[0, 1:2, :] = jnp.sum(d_raw, axis=0, keepdims=True)


def strand(*shape):
    return pl.BlockSpec((1,) + shape, lambda s: (s,) + (0,) * len(shape))


def shared(*shape):
    return pl.BlockSpec(shape, lambda s: (0,) * len(shape))


STATE = pl.BlockSpec((H, P_SIZE, NS), lambda s: (0, s, 0))


def like(dtype, *shape):
    return jax.ShapeDtypeStruct(shape, dtype)


def strand_call(kernel, name, in_specs, out_specs, out_shape, scratch=(), flops=2000000000):
    return pl.pallas_call(
        kernel, grid=(2,), in_specs=in_specs, out_specs=out_specs, out_shape=out_shape,
        scratch_shapes=list(scratch), name=name,
        cost_estimate=pl.CostEstimate(flops=flops, bytes_accessed=10000000, transcendentals=0))


def flipped(block):
    turn = (iota((128, 128), 0) + iota((128, 128), 1) == 127).astype(f32).astype(bf16)
    rows = dot(turn, block).astype(bf16)
    parts = [dot(rows[:, 128 * j : 128 * j + 128], turn) for j in range(15, -1, -1)]
    return jnp.concatenate(parts, 1)


def flip_kernel(keep, got, out, mine, theirs):
    out[0] = keep[...]
    out[1] = flipped(got[...]).astype(bf16)
    core = lax.rem(lax.axis_index("dp"), 2)
    for s in range(2):
        for half in range(2):
            rows, cols = slice(Q * s, Q * s + Q), slice(512 * half, 512 * half + 512)
            mine[rows, cols] = out[s, :, pl.ds(pl.multiple_of((2 * half + core) * 512, 128), 512)]
            theirs[rows, cols] = out[s, :, pl.ds(pl.multiple_of((2 * half + 1 - core) * 512, 128), 512)]


def mix_kernel(own, got, out):
    out[...] = (own[...].astype(f32) + flipped(got[...])).astype(bf16)


def whole_call(kernel, name, out_shape, *args):
    vmem = pl.BlockSpec(memory_space=pltpu.VMEM)
    return pl.pallas_call(
        kernel, out_shape=out_shape, in_specs=[vmem] * len(args), out_specs=jax.tree.map(lambda _: vmem, out_shape), name=name,
        cost_estimate=pl.CostEstimate(flops=200000000, bytes_accessed=2000000, transcendentals=0))(*args)


def mirror(value):
    return lax.ppermute(value, "ctx", [(i, N_CTX - 1 - i) for i in range(N_CTX)])


def other_core(value):
    return lax.ppermute(value, "dp", [(i, i ^ 1) for i in range(4)])


def body(projections, dt_raw, a_log, dt_bias, skip_gain, norm_gain, w_out, base_ids, cotangent):
    keep = cotangent * (base_ids != 4).astype(bf16)[:, None]
    got_keep = mirror(keep)
    proj, tok = strand(Q, 2 * DI + 2 * NS), strand(Q, H)
    tok_t, wide = strand(H, Q), strand(Q, DI)
    row, lane = shared(1, H), shared(1, DI)
    skip, gain = jnp.repeat(skip_gain, P_SIZE)[None], norm_gain[None]
    state, factor, dt, run, dt_t, run_t = strand_call(
        summary_kernel, "summary", [proj, tok, row, row],
        [STATE, pl.BlockSpec((H, 8, NS), lambda s: (0, s, 0)), tok, tok, tok_t, tok_t],
        [like(bf16, H, 2 * P_SIZE, NS), like(f32, H, 16, NS), like(f32, 2, Q, H), like(f32, 2, Q, H),
         like(f32, 2, H, Q), like(f32, 2, H, Q)],
    )(projections, dt_raw, a_log[None], dt_bias[None])
    states = like(bf16, H, 2 * P_SIZE, NS)
    entering, decays, local, spread, mixing = exchange_call(
        forward_exchange, "forward_exchange", 1,
        [states, like(f32, H, 16, NS), like(f32, 2, Q, DI)] + [like(bf16, 2, PAIRS, Q, 2 * Q)] * 2,
        scan_scratch(), state, factor, projections, run, dt_t, run_t)
    d_out, grads, grads_away = whole_call(
        flip_kernel, "flip_keep", [like(bf16, 2, Q, DI)] + [like(bf16, 2 * Q, DI // 2)] * 2, keep, got_keep)
    spread_spec = strand(PAIRS, Q, 2 * Q)
    normed, y = strand_call(
        forward_kernel, "forward", [proj, tok, wide, STATE, lane, lane], [wide, wide],
        [like(bf16, 2, Q, DI), like(f32, 2, Q, DI)],
    )(projections, run, local, entering, skip, gain)
    strand_out = jnp.einsum("srk,dk->srd", normed, w_out, preferred_element_type=f32).astype(bf16)
    moved = mirror(strand_out[1])
    d_normed = jnp.einsum("srd,dk->srk", d_out, w_out, preferred_element_type=f32).astype(bf16)
    d_gate, d_x, d_entering, d_write, d_read, gains, from_y, from_x = strand_call(
        backward_kernel, "backward", [proj, wide, wide, tok, spread_spec, spread_spec, STATE, lane, lane],
        [wide, wide, STATE, strand(Q, NS), strand(Q, NS), strand(2, DI), tok, tok],
        [like(bf16, 2, Q, DI), like(f32, 2, Q, DI), like(bf16, H, 2 * P_SIZE, NS), like(f32, 2, Q, NS),
         like(bf16, 2, Q, NS), like(f32, 2, 2, DI), like(f32, 2, Q, H), like(f32, 2, Q, H)],
        [pltpu.VMEM((Q, DI), bf16), pltpu.VMEM((Q, DI), f32)],
    )(projections, y, d_normed, run, spread, mixing, entering, skip, gain)
    flat = normed.reshape(2 * Q, DI)
    leaving, partial = exchange_call(
        backward_exchange, "backward_exchange", 2, [states, like(bf16, 4, 4, 4, 16, DI)], scan_scratch(),
        d_entering, decays, grads, other_core(grads_away), flat, other_core(flat))
    mixed_out = whole_call(mix_kernel, "mix", like(bf16, Q, DI), strand_out[0], moved)
    d_proj, d_dt, sums = strand_call(
        finish_kernel, "finish",
        [proj, tok, tok, tok, STATE, STATE, tok, tok, wide, wide, strand(Q, NS), strand(Q, NS), row, row],
        [proj, tok, strand(2, H)],
        [like(bf16, 2, Q, 2 * DI + 2 * NS), like(bf16, 2, Q, H), like(f32, 2, 2, H)],
    )(projections, dt_raw, dt, run, leaving, entering, from_y, from_x, d_x, d_gate, d_write, d_read,
      a_log[None], dt_bias[None])
    gains = jnp.sum(gains, axis=0)
    d_skip = jnp.sum(gains[1].reshape(H, P_SIZE), axis=1)
    small = jnp.concatenate([gains[0], jnp.sum(sums, axis=0).reshape(-1), d_skip, jnp.zeros((928,), f32)])
    summed, d_w_out = exchange_call(
        last_exchange, "last_exchange", 3, [like(f32, 24, 128), like(f32, 16, DI)],
        sum_scratch((24, 128)) + scatter_scratch(), small.reshape(24, 128), partial)
    summed = summed.reshape(-1)
    return (mixed_out, d_proj, d_dt, d_w_out, summed[2048 : 2048 + 96].reshape(3, 32), summed[:2048])


def solution(mesh):
    placed = (
        P(None, ("dp", "ctx"), None),
        P(None, ("dp", "ctx"), None),
        P(),
        P(),
        P(),
        P(),
        P(),
        P(("dp", "ctx")),
        P(("dp", "ctx"), None),
    )
    return jax.shard_map(
        body,
        mesh=mesh,
        in_specs=placed,
        out_specs=(
            P(("dp", "ctx"), None),
            P(None, ("dp", "ctx"), None),
            P(None, ("dp", "ctx"), None),
            P(("dp", "ctx"), None),
            P(),
            P(),
        ),
        check_vma=False,
    )
```

```python
import functools

import jax
import jax.numpy as jnp
from jax import lax
from jax.experimental import pallas as pl
from jax.experimental.pallas import tpu as pltpu
from jax.sharding import PartitionSpec as P

MESH = pl.DeviceIdType.MESH
N_CTX = 32


CUTS = ((0, 768), (768, 1408), (1408, 2048))


def place():
    dp, ctx = lax.axis_index("dp"), lax.axis_index("ctx")
    x_lo, core = dp // 2, lax.rem(dp, 2)
    x_hi, z, y = ctx // 16, lax.rem(ctx // 4, 4), lax.rem(ctx, 4)
    return dp, core, {"x": x_lo * 2 + x_hi, "z": z, "y": y}


def line_peer(axis, k):
    dp, core, at = place()
    there = lax.rem(at[axis] + k, 4)
    x = there if axis == "x" else at["x"]
    z = there if axis == "z" else at["z"]
    y = there if axis == "y" else at["y"]
    return there, ((x // 2) * 2 + core, lax.rem(x, 2) * 16 + z * 4 + y)


def scatter_steps(s_ref, out_ref, scratch):
    (ra0, ra1, ra2, sa0, sa1, sa2, rb0, rb1, rb2, sb0, sb1, sb2, rc0, rc1, rc2, send_sem, recv_sem) = scratch
    _, _, at = place()
    cols = [pl.ds(a, b - a) for a, b in CUTS]
    axes = (("y", "z", "x"), ("z", "x", "y"), ("x", "y", "z"))

    def send(stage, part, k, pick, dst):
        there, device = line_peer(axes[part][stage], k)
        index = (stage * 3 + part) * 3 + k - 1
        copy = pltpu.make_async_remote_copy(
            src_ref=pick(there), dst_ref=dst.at[k - 1],
            send_sem=send_sem.at[index], recv_sem=recv_sem.at[index],
            device_id=device, device_id_type=MESH)
        copy.start()
        return copy

    def add(mine, recv, i):
        total = mine.astype(jnp.float32)
        for k in range(3):
            total = total + recv[(k,) + i].astype(jnp.float32)
        return total

    pending = {}

    def begin():
        picks = (
            lambda t: s_ref.at[:, :, t, :, cols[0]],
            lambda t: s_ref.at[:, t, :, :, cols[1]],
            lambda t: s_ref.at[t, :, :, :, cols[2]],
        )
        pending[0] = [[send(0, p, k, picks[p], (ra0, ra1, ra2)[p]) for k in (2, 1, 3)] for p in range(3)]

    def second():
        pending[1] = []
        for p in range(3):
            for copy in pending[0][p]:
                copy.wait()
            ra, sa = (ra0, ra1, ra2)[p], (sa0, sa1, sa2)[p]

            def step(i, c, p=p, ra=ra, sa=sa):
                a, b = i // 4, lax.rem(i, 4)
                if p == 0:
                    mine = s_ref[a, b, at["y"], :, cols[0]]
                elif p == 1:
                    mine = s_ref[a, at["z"], b, :, cols[1]]
                else:
                    mine = s_ref[at["x"], a, b, :, cols[2]]
                sa[a, b] = add(mine, ra, (a, b)).astype(jnp.bfloat16)
                return c

            lax.fori_loop(0, 16, step, 0)
            pick = (lambda t: sa0.at[:, t], lambda t: sa1.at[t], lambda t: sa2.at[:, t])[p]
            pending[1].append([send(1, p, k, pick, (rb0, rb1, rb2)[p]) for k in (2, 1, 3)])

    def third():
        pending[2] = []
        for p in range(3):
            for copy in pending[1][p]:
                copy.wait()
            rb, sb = (rb0, rb1, rb2)[p], (sb0, sb1, sb2)[p]
            for i in range(4):
                mine = (lambda: sa0[i, at["z"]], lambda: sa1[at["x"], i], lambda: sa2[i, at["y"]])[p]()
                sb[i] = add(mine, rb, (i,)).astype(jnp.bfloat16)
            pending[2].append([send(2, p, k, lambda t, sb=sb: sb.at[t], (rc0, rc1, rc2)[p]) for k in (2, 1, 3)])

    def end():
        for p in range(3):
            for copy in pending[2][p]:
                copy.wait()
            sb, rc = (sb0, sb1, sb2)[p], (rc0, rc1, rc2)[p]
            out_ref[:, cols[p]] = add(sb[at[axes[p][2]]], rc, ())

    return begin, second, third, end


def scan_steps(backward, s_ref, dec_ref, out_ref, got_dec, scratch):
    got, pre, send_a, recv_a, send_d, recv_d, send_b, recv_b, own_sem = scratch
    me = lax.axis_index("ctx")

    def peer_of(k):
        return lax.rem(me + k * 5, N_CTX)

    def state_copy(src, dst, send, recv, strand_at):
        rows = pl.ds(0, 2 * P_SIZE)

        def make(k):
            return pltpu.make_async_remote_copy(
                src_ref=src.at[peer_of(k), rows], dst_ref=dst.at[me, rows],
                send_sem=send.at[strand_at, k], recv_sem=recv.at[strand_at, k],
                device_id={"ctx": peer_of(k)}, device_id_type=MESH)
        return make

    def copy_d(k):
        return pltpu.make_async_remote_copy(
            src_ref=dec_ref.at[peer_of(k)], dst_ref=got_dec.at[me], send_sem=send_d.at[k], recv_sem=recv_d.at[k],
            device_id={"ctx": peer_of(k)}, device_id_type=MESH)

    copy_a = state_copy(s_ref, got, send_a, recv_a, 0)
    copy_b = state_copy(pre, out_ref, send_b, recv_b, 0)

    def start(make):
        def step(k, c):
            make(k).start()
            return c
        lax.fori_loop(1, N_CTX, step, 0)

    def finish(make):
        def step(k, c):
            make(k).wait()
            return c
        lax.fori_loop(1, N_CTX, step, 0)

    def begin():
        if not backward:
            start(copy_d)
        start(copy_a)
        own = pltpu.make_async_copy(s_ref.at[me], got.at[me], own_sem.at[0])
        own.start()
        own.wait()
        if not backward:
            own_d = pltpu.make_async_copy(dec_ref.at[me], got_dec.at[me], own_sem.at[1])
            own_d.start()
            own_d.wait()

    def turn():
        if not backward:
            finish(copy_d)
        decays = dec_ref if backward else got_dec
        finish(copy_a)
        for i in range(2):
            rows = slice(P_SIZE * i, P_SIZE * i + P_SIZE)

            def fold(n, carry, i=i, rows=rows):
                at = N_CTX - 1 - n if backward else n
                pre[at, rows, :] = carry.astype(jnp.bfloat16)
                return decays[at, 8 * i : 8 * i + 1, :] * carry + got[at, rows, :].astype(jnp.float32)

            lax.fori_loop(0, N_CTX, fold, jnp.zeros((P_SIZE, NS), jnp.float32))
        start(copy_b)

    def end():
        own = pltpu.make_async_copy(pre.at[me], out_ref.at[me], own_sem.at[2])
        own.start()
        own.wait()
        finish(copy_b)

    return begin, turn, end


def greet_line():
    me = lax.axis_index("ctx")
    barrier = pltpu.get_barrier_semaphore()

    def step(k, c):
        pl.semaphore_signal(barrier, inc=1, device_id={"ctx": lax.rem(me + k, N_CTX)}, device_id_type=MESH)
        return c

    lax.fori_loop(1, N_CTX, step, 0)
    pl.semaphore_wait(barrier, N_CTX - 1)


def forward_exchange(s_ref, dec_ref, proj, run, dt_t, run_t, out_ref, got_dec, local, spread_out, mix_out, *scratch):
    begin, turn, end = scan_steps(False, s_ref, dec_ref, out_ref, got_dec, scratch)
    greet_line()
    begin()

    def block(s, c):
        local_outputs(s, proj, run, dt_t, run_t, local, spread_out, mix_out)
        return c

    lax.fori_loop(0, 2, block, 0)
    turn()
    end()


def backward_exchange(s_ref, dec_ref, grads, grads_other, normed, normed_other, out_ref, partial, *scratch):
    begin, turn, end = scan_steps(True, s_ref, dec_ref, out_ref, None, scratch)
    greet_line()
    begin()

    def rows(i, c):
        at = pl.ds(pl.multiple_of(i * 256, 128), 256)
        total = dot(grads[:, at], normed[...], ROWS) + dot(grads_other[:, at], normed_other[...], ROWS)
        partial[i] = total.astype(jnp.bfloat16).reshape(4, 4, 16, 2048)
        return c

    lax.fori_loop(0, 4, rows, 0)
    turn()
    end()


def last_exchange(v_ref, weight, out_v, d_weight, plane, line, part, send_a, recv_a, send_b, recv_b, *scratch):
    w_begin, w_second, w_third, w_end = scatter_steps(weight, d_weight, scratch)
    dp, ctx = lax.axis_index("dp"), lax.axis_index("ctx")
    q, x_hi = lax.rem(ctx, 16), ctx // 16
    e = x_hi * 4 + dp

    def peer_a(k):
        return (dp, x_hi * 16 + lax.rem(q + k, 16))

    def peer_b(k):
        there = lax.rem(e + k, 8)
        return (lax.rem(there, 4), (there // 4) * 16 + q)

    barrier = pltpu.get_barrier_semaphore()
    peers = [peer_a(k) for k in range(1, 16)] + [peer_b(k) for k in range(1, 8)]
    peers += [line_peer(axis, k)[1] for axis in "xyz" for k in (1, 2, 3)]
    for device in peers:
        pl.semaphore_signal(barrier, inc=1, device_id=device, device_id_type=MESH)
    pl.semaphore_wait(barrier, len(peers))

    def copy_a(k):
        return pltpu.make_async_remote_copy(
            src_ref=v_ref, dst_ref=plane.at[q], send_sem=send_a.at[k], recv_sem=recv_a.at[k],
            device_id=peer_a(k), device_id_type=MESH)

    def copy_b(k):
        return pltpu.make_async_remote_copy(
            src_ref=part, dst_ref=line.at[e], send_sem=send_b.at[k], recv_sem=recv_b.at[k],
            device_id=peer_b(k), device_id_type=MESH)

    first = [copy_a(k) for k in range(1, 16)]
    for copy in first:
        copy.start()
    w_begin()
    plane[q] = v_ref[...]
    for copy in first:
        copy.wait()
    total = plane[0]
    for i in range(1, 16):
        total = total + plane[i]
    part[...] = total
    line[e] = total
    second = [copy_b(k) for k in range(1, 8)]
    for copy in second:
        copy.start()
    w_second()
    for copy in second:
        copy.wait()
    total = line[0]
    for i in range(1, 8):
        total = total + line[i]
    out_v[...] = total
    w_third()
    w_end()


def exchange_call(kernel, name, collective_id, out_shape, scratch, *args):
    vmem = pl.BlockSpec(memory_space=pltpu.VMEM)
    return pl.pallas_call(
        kernel, out_shape=out_shape, in_specs=[vmem] * len(args), out_specs=[vmem] * len(out_shape),
        scratch_shapes=scratch, name=name,
        compiler_params=pltpu.CompilerParams(collective_id=collective_id, has_side_effects=True),
        cost_estimate=pl.CostEstimate(flops=1000000, bytes_accessed=4000000, transcendentals=0))(*args)


def scan_scratch():
    dma = pltpu.SemaphoreType.DMA
    state = pltpu.VMEM((N_CTX, 128, 128), jnp.bfloat16)
    pairs, singles = dma((2, N_CTX)), dma((N_CTX,))
    return [state, state, pairs, pairs, singles, singles, pairs, pairs, dma((3,))]


def sum_scratch(shape):
    dma = pltpu.SemaphoreType.DMA
    return [
        pltpu.VMEM((16,) + shape, jnp.float32), pltpu.VMEM((8,) + shape, jnp.float32),
        pltpu.VMEM(shape, jnp.float32), dma((16,)), dma((16,)), dma((8,)), dma((8,))]


def scatter_scratch():
    widths = [b - a for a, b in CUTS]
    shapes = ((3, 4, 4, 16), (4, 4, 16), (3, 4, 16), (4, 16), (3, 16))
    scratch = [pltpu.VMEM(shape + (w,), jnp.bfloat16) for shape in shapes for w in widths]
    return scratch + [pltpu.SemaphoreType.DMA((27,)), pltpu.SemaphoreType.DMA((27,))]


H = 32
P_SIZE = 64
NS = 128
DI = 2048
Q = 128
PAIRS = 16
B_AT = 2 * DI
C_AT = 2 * DI + NS
bf16 = jnp.bfloat16
f32 = jnp.float32
precise = lax.Precision.HIGHEST


def dot(a, b, dims=((1,), (0,)), precision=None):
    return lax.dot_general(a, b, (dims, ((), ())), precision=precision, preferred_element_type=f32)


ROWS = ((0,), (0,))
LANES = ((1,), (1,))


def iota(shape, axis):
    return lax.broadcasted_iota(jnp.int32, shape, axis)


def head_map():
    return (iota((H, DI), 0) == iota((H, DI), 1) // P_SIZE).astype(f32).astype(bf16)


def expand(value, heads):
    high = value.astype(bf16)
    low = (value - high.astype(f32)).astype(bf16)
    return dot(high, heads) + dot(low, heads)


def per_head(value, heads):
    return dot(value.astype(bf16), heads, LANES)


def softplus(value):
    return jnp.maximum(value, 0.0) + jnp.log1p(jnp.exp(-jnp.abs(value)))


def sigmoid(value):
    return 1.0 / (1.0 + jnp.exp(-value))


def tril():
    return iota((Q, Q), 0) >= iota((Q, Q), 1)


def half_masks():
    left = (iota((Q, 128), 1) < P_SIZE).astype(f32)
    return left.astype(bf16), (1.0 - left).astype(bf16)


def summary_kernel(proj, dt_raw, a_log, bias, state, decay, dt_out, run_out, dt_t_out, run_t_out):
    lower = tril().astype(f32)
    same = (iota((Q, Q), 0) == iota((Q, Q), 1)).astype(f32)
    dt = softplus(dt_raw[0].astype(f32) + bias[...])
    run = dot(lower, -jnp.exp(a_log[...]) * dt, precision=precise)
    run_t = dot(run, same, ROWS, precision=precise)
    dt_out[0] = dt
    run_out[0] = run
    dt_t_out[0] = dot(dt, same, ROWS, precision=precise)
    run_t_out[0] = run_t
    weight = jnp.exp(run[Q - 1 : Q, :] - run) * dt
    weighed = (expand(weight, head_map()) * proj[0, :, DI:B_AT].astype(f32)).astype(bf16)
    total = dot(weighed, proj[0, :, B_AT:C_AT], ROWS)
    state[...] = total.astype(bf16).reshape(H, P_SIZE, NS)
    left = jnp.exp(run_t[:, Q - 1 : Q])
    for h in range(H):
        decay[h] = jnp.broadcast_to(left[h : h + 1, :], (8, 128))


def local_outputs(s, proj, run, dt_t, run_t, local, spread_out, mix_out):
    affinity = dot(proj[s, :, C_AT:], proj[s, :, B_AT:C_AT], LANES)
    affinity = jnp.concatenate([affinity, affinity], 1)
    causal = tril()
    left, right = half_masks()
    for j in range(PAIRS):
        cols = slice(DI + 128 * j, DI + 128 * j + 128)
        both = []
        for h in (2 * j, 2 * j + 1):
            gap = run[s, :, h : h + 1] - run_t[s, h : h + 1, :]
            both.append(jnp.exp(jnp.where(causal, gap, -1e30)) * dt_t[s, h : h + 1, :])
        spread = jnp.concatenate(both, 1)
        spread_out[s, j] = spread.astype(bf16)
        values = proj[s, :, cols]
        stacked = jnp.concatenate([values * left, values * right], 0)
        mixing = (spread * affinity).astype(bf16)
        mix_out[s, j] = mixing
        local[s, :, 128 * j : 128 * j + 128] = dot(mixing, stacked)


def forward_kernel(proj, run, local, entering, skip, gain, normed, y_out):
    carried = dot(proj[0, :, C_AT:], entering[...].reshape(DI, NS), LANES)
    grown = expand(jnp.exp(run[0]), head_map())
    y = local[0] + grown * carried + skip[...] * proj[0, :, DI:B_AT].astype(f32)
    y_out[0] = y
    gate = proj[0, :, :DI].astype(f32)
    gated = y * gate * sigmoid(gate)
    inv = lax.rsqrt(jnp.mean(gated * gated, axis=1, keepdims=True) + 1e-05)
    normed[0] = (gated * inv * gain[...]).astype(bf16)


def backward_kernel(proj, y_in, d_normed, run, spread_in, mix_in, entering, skip, gain,
                    d_gate, d_x, d_entering, d_write, d_read, gains, from_y, from_x, dy_keep, dx_keep):
    heads = head_map()
    gate = proj[0, :, :DI].astype(f32)
    y = y_in[0]
    sig = sigmoid(gate)
    silu = gate * sig
    gated = y * silu
    inv = lax.rsqrt(jnp.mean(gated * gated, axis=1, keepdims=True) + 1e-05)
    dn = d_normed[0].astype(f32)
    gains[0, 0:1, :] = jnp.sum(dn * (gated * inv), axis=0, keepdims=True)
    up = dn * gain[...]
    pull = jnp.mean(up * gated, axis=1, keepdims=True) * (inv * inv * inv)
    d_gated = inv * up - gated * pull
    dy = d_gated * silu
    d_gate[0] = (d_gated * y * (sig * (1.0 + gate * (1.0 - sig)))).astype(bf16)
    values = proj[0, :, DI:B_AT].astype(f32)
    gains[0, 1:2, :] = jnp.sum(dy * values, axis=0, keepdims=True)
    dy_keep[...] = dy.astype(bf16)
    from_y[0] = per_head(dy_keep[...].astype(f32) * (y - skip[...] * values), heads)
    grown = (expand(jnp.exp(run[0]), heads) * dy).astype(bf16)
    write, read = proj[0, :, B_AT:C_AT], proj[0, :, C_AT:]
    state = entering[...].reshape(DI, NS)
    d_entering[...] = dot(grown, read, ROWS).astype(bf16).reshape(H, P_SIZE, NS)
    d_c = dot(grown, state)
    left, right = half_masks()
    first = iota((Q, 128), 1) < P_SIZE
    d_aff = jnp.zeros((Q, Q), f32)
    for j in range(PAIRS):
        cols = slice(128 * j, 128 * j + 128)
        dyp = dy_keep[:, cols]
        x = proj[0, :, DI + 128 * j : DI + 128 * j + 128]
        stacked = jnp.concatenate([x * left, x * right], 0)
        d_mix = dot(dyp, stacked, LANES) * spread_in[0, j].astype(f32)
        d_aff = d_aff + d_mix[:, :Q] + d_mix[:, Q:]
        back = dot(mix_in[0, j], dyp, ROWS)
        dx_keep[:, cols] = jnp.where(first, back[:Q], back[Q:])
    d_aff = d_aff.astype(bf16)
    d_read[0] = (d_c + dot(d_aff, write)).astype(bf16)
    d_write[0] = dot(d_aff, read, ROWS)
    dx = dx_keep[...]
    from_x[0] = per_head(values * dx, heads)
    d_x[0] = dx + skip[...] * dy


def finish_kernel(proj, dt_raw, dt_in, run_in, leaving, entering, from_y, from_x, d_x, d_gate, d_write, d_read,
                  a_log, bias, d_proj, d_dt, sums):
    heads = head_map()
    rate = jnp.exp(a_log[...])
    dt, run = dt_in[0], run_in[0]
    last = run[Q - 1 : Q, :]
    weight = expand(jnp.exp(last - run) * dt, heads)
    values = proj[0, :, DI:B_AT].astype(f32)
    out = leaving[...].reshape(DI, NS)
    d_state = weight * dot(proj[0, :, B_AT:C_AT], out, LANES)
    d_b = d_write[0] + dot((weight * values).astype(bf16), out)
    d_proj[0, :, :DI] = d_gate[0]
    d_proj[0, :, DI:B_AT] = (d_x[0] + d_state).astype(bf16)
    d_proj[0, :, B_AT:C_AT] = d_b.astype(bf16)
    d_proj[0, :, C_AT:] = d_read[0]
    from_state = per_head(values * d_state, heads)
    total = from_x[0] + from_state
    meet = jnp.sum(entering[...].astype(f32) * leaving[...].astype(f32), axis=1)
    meet = dot(jnp.ones((8, NS), f32), meet, LANES, precision=precise)[0:1, :]
    d_last = jnp.exp(last) * meet + jnp.sum(from_state, axis=0, keepdims=True)
    upper = (iota((Q, Q), 0) <= iota((Q, Q), 1)).astype(f32)
    d_log = dot(upper, from_y[0] - total, precision=precise) + d_last
    d_step = total / dt - rate * d_log
    d_raw = d_step * sigmoid(dt_raw[0].astype(f32) + bias[...])
    d_dt[0] = d_raw.astype(bf16)
    sums[0, 0:1, :] = jnp.sum(d_log * (-rate * dt), axis=0, keepdims=True)
    sums[0, 1:2, :] = jnp.sum(d_raw, axis=0, keepdims=True)


def strand(*shape):
    return pl.BlockSpec((1,) + shape, lambda s: (s,) + (0,) * len(shape))


def shared(*shape):
    return pl.BlockSpec(shape, lambda s: (0,) * len(shape))


STATE = pl.BlockSpec((H, P_SIZE, NS), lambda s: (0, s, 0))


def like(dtype, *shape):
    return jax.ShapeDtypeStruct(shape, dtype)


def strand_call(kernel, name, in_specs, out_specs, out_shape, scratch=(), flops=2000000000):
    return pl.pallas_call(
        kernel, grid=(2,), in_specs=in_specs, out_specs=out_specs, out_shape=out_shape,
        scratch_shapes=list(scratch), name=name,
        cost_estimate=pl.CostEstimate(flops=flops, bytes_accessed=10000000, transcendentals=0))


def flipped(block):
    turn = (iota((128, 128), 0) + iota((128, 128), 1) == 127).astype(f32).astype(bf16)
    rows = dot(turn, block).astype(bf16)
    parts = [dot(rows[:, 128 * j : 128 * j + 128], turn) for j in range(15, -1, -1)]
    return jnp.concatenate(parts, 1)


def flip_kernel(keep, got, out, mine, theirs):
    out[0] = keep[...]
    out[1] = flipped(got[...]).astype(bf16)
    core = lax.rem(lax.axis_index("dp"), 2)
    for s in range(2):
        for half in range(2):
            rows, cols = slice(Q * s, Q * s + Q), slice(512 * half, 512 * half + 512)
            mine[rows, cols] = out[s, :, pl.ds(pl.multiple_of((2 * half + core) * 512, 128), 512)]
            theirs[rows, cols] = out[s, :, pl.ds(pl.multiple_of((2 * half + 1 - core) * 512, 128), 512)]


def mix_kernel(own, got, out):
    out[...] = (own[...].astype(f32) + flipped(got[...])).astype(bf16)


def whole_call(kernel, name, out_shape, *args):
    vmem = pl.BlockSpec(memory_space=pltpu.VMEM)
    return pl.pallas_call(
        kernel, out_shape=out_shape, in_specs=[vmem] * len(args), out_specs=jax.tree.map(lambda _: vmem, out_shape), name=name,
        cost_estimate=pl.CostEstimate(flops=200000000, bytes_accessed=2000000, transcendentals=0))(*args)


def mirror(value):
    return lax.ppermute(value, "ctx", [(i, N_CTX - 1 - i) for i in range(N_CTX)])


def other_core(value):
    return lax.ppermute(value, "dp", [(i, i ^ 1) for i in range(4)])


def body(projections, dt_raw, a_log, dt_bias, skip_gain, norm_gain, w_out, base_ids, cotangent):
    keep = cotangent * (base_ids != 4).astype(bf16)[:, None]
    got_keep = mirror(keep)
    proj, tok = strand(Q, 2 * DI + 2 * NS), strand(Q, H)
    tok_t, wide = strand(H, Q), strand(Q, DI)
    row, lane = shared(1, H), shared(1, DI)
    skip, gain = jnp.repeat(skip_gain, P_SIZE)[None], norm_gain[None]
    state, factor, dt, run, dt_t, run_t = strand_call(
        summary_kernel, "summary", [proj, tok, row, row],
        [STATE, pl.BlockSpec((H, 8, NS), lambda s: (0, s, 0)), tok, tok, tok_t, tok_t],
        [like(bf16, H, 2 * P_SIZE, NS), like(f32, H, 16, NS), like(f32, 2, Q, H), like(f32, 2, Q, H),
         like(f32, 2, H, Q), like(f32, 2, H, Q)],
    )(projections, dt_raw, a_log[None], dt_bias[None])
    states = like(bf16, H, 2 * P_SIZE, NS)
    entering, decays, local, spread, mixing = exchange_call(
        forward_exchange, "forward_exchange", 1,
        [states, like(f32, H, 16, NS), like(f32, 2, Q, DI)] + [like(bf16, 2, PAIRS, Q, 2 * Q)] * 2,
        scan_scratch(), state, factor, projections, run, dt_t, run_t)
    d_out, grads, grads_away = whole_call(
        flip_kernel, "flip_keep", [like(bf16, 2, Q, DI)] + [like(bf16, 2 * Q, DI // 2)] * 2, keep, got_keep)
    spread_spec = strand(PAIRS, Q, 2 * Q)
    normed, y = strand_call(
        forward_kernel, "forward", [proj, tok, wide, STATE, lane, lane], [wide, wide],
        [like(bf16, 2, Q, DI), like(f32, 2, Q, DI)],
    )(projections, run, local, entering, skip, gain)
    strand_out = jnp.einsum("srk,dk->srd", normed, w_out, preferred_element_type=f32).astype(bf16)
    moved = mirror(strand_out[1])
    d_normed = jnp.einsum("srd,dk->srk", d_out, w_out, preferred_element_type=f32).astype(bf16)
    d_gate, d_x, d_entering, d_write, d_read, gains, from_y, from_x = strand_call(
        backward_kernel, "backward", [proj, wide, wide, tok, spread_spec, spread_spec, STATE, lane, lane],
        [wide, wide, STATE, strand(Q, NS), strand(Q, NS), strand(2, DI), tok, tok],
        [like(bf16, 2, Q, DI), like(f32, 2, Q, DI), like(bf16, H, 2 * P_SIZE, NS), like(f32, 2, Q, NS),
         like(bf16, 2, Q, NS), like(f32, 2, 2, DI), like(f32, 2, Q, H), like(f32, 2, Q, H)],
        [pltpu.VMEM((Q, DI), bf16), pltpu.VMEM((Q, DI), f32)],
    )(projections, y, d_normed, run, spread, mixing, entering, skip, gain)
    flat = normed.reshape(2 * Q, DI)
    leaving, partial = exchange_call(
        backward_exchange, "backward_exchange", 2, [states, like(bf16, 4, 4, 4, 16, DI)], scan_scratch(),
        d_entering, decays, grads, other_core(grads_away), flat, other_core(flat))
    mixed_out = whole_call(mix_kernel, "mix", like(bf16, Q, DI), strand_out[0], moved)
    d_proj, d_dt, sums = strand_call(
        finish_kernel, "finish",
        [proj, tok, tok, tok, STATE, STATE, tok, tok, wide, wide, strand(Q, NS), strand(Q, NS), row, row],
        [proj, tok, strand(2, H)],
        [like(bf16, 2, Q, 2 * DI + 2 * NS), like(bf16, 2, Q, H), like(f32, 2, 2, H)],
    )(projections, dt_raw, dt, run, leaving, entering, from_y, from_x, d_x, d_gate, d_write, d_read,
      a_log[None], dt_bias[None])
    gains = jnp.sum(gains, axis=0)
    d_skip = jnp.sum(gains[1].reshape(H, P_SIZE), axis=1)
    small = jnp.concatenate([gains[0], jnp.sum(sums, axis=0).reshape(-1), d_skip, jnp.zeros((928,), f32)])
    summed, d_w_out = exchange_call(
        last_exchange, "last_exchange", 3, [like(f32, 24, 128), like(f32, 16, DI)],
        sum_scratch((24, 128)) + scatter_scratch(), small.reshape(24, 128), partial)
    summed = summed.reshape(-1)
    return (mixed_out, d_proj, d_dt, d_w_out, summed[2048 : 2048 + 96].reshape(3, 32), summed[:2048])


def solution(mesh):
    placed = (
        P(None, ("dp", "ctx"), None),
        P(None, ("dp", "ctx"), None),
        P(),
        P(),
        P(),
        P(),
        P(),
        P(("dp", "ctx")),
        P(("dp", "ctx"), None),
    )
    return jax.shard_map(
        body,
        mesh=mesh,
        in_specs=placed,
        out_specs=(
            P(("dp", "ctx"), None),
            P(None, ("dp", "ctx"), None),
            P(None, ("dp", "ctx"), None),
            P(("dp", "ctx"), None),
            P(),
            P(),
        ),
        check_vma=False,
    )
```
